512 devices in a mesh: seq: 32 (over z_hi, y), dp: 16 (over z_lo, x, core).
Axes of the slice: x: 4, y: 8, z: 8 (z_hi: 4, z_lo: 2; z = z_hi * 2 + z_lo), core: 2. Of those that a mesh axis runs over, the one named last changes fastest.
Arguments:
- queries: bfloat16 [16, 4096, 1024], P('dp', 'seq'), may hold values from -150 to 150
- key_states: bfloat16 [16, 4096, 1024], P('dp', 'seq'), may hold values from -6 to 6
- values: bfloat16 [16, 4096, 1024], P('dp', 'seq'), may hold values from -6 to 6
- w_out: bfloat16 [1024, 1024], replicated, may hold values from -0.1875 to 0.1875
- cotangent: bfloat16 [16, 4096, 1024], P('dp', 'seq'), may hold values from -6 to 6
- neighbours: int32 [16, 32, 2], P('dp', 'seq'), may hold values from 0 to 31, as said below
- counts: int32 [16, 32], P('dp', 'seq'), may hold values from 1 to 2
Outputs:
- output: bfloat16 [16, 4096, 1024], P('dp', 'seq')
- grad_queries: bfloat16 [16, 4096, 1024], P('dp', 'seq')
- grad_keys: bfloat16 [16, 4096, 1024], P('dp', 'seq')
- grad_values: bfloat16 [16, 4096, 1024], P('dp', 'seq')
- grad_w_out: float32 [1024, 1024], P(('seq', 'dp'))
The draws below stay inside these ranges and needn't reach their ends.
Inputs may be any that keep to these rules, and one draw needn't show every extreme that they name: `neighbours`: entries j < counts[s, p] of patch p's list are distinct patches other than p, at most 1 patches away from p; the later entries equal p.
All inputs are finite; a program needn't handle non-finite values.
Results may differ from the reference program's by a relative error of at most 0.029.
Values may be sent and summed in bfloat16 or wider, within the bound.
A program may use at most 64 MiB of HBM per device.

```python
import math
import jax
import jax.numpy as jnp
from jax import lax

PATCH = 128
HEADS = 8
HD = 128
DW = 1024
NB = 2
REACH = 1
HW = 1024
NPATCH = 32
SEQLEN = 4096
SAMPLES = 16


def query_key_pair(key):
    base_key = jax.random.fold_in(key, 7)
    draw_one, draw_two = jax.random.split(base_key, 2)
    full_shape = (SAMPLES, SEQLEN, HEADS * HD)
    drawn_keys = jnp.clip(jax.random.normal(draw_one, full_shape, jnp.float32), -5.0, 5.0)
    key_out = drawn_keys
    query_out = 2.0 * jnp.clip(jax.random.normal(draw_two, full_shape, jnp.float32), -5.0, 5.0)
    return (query_out, key_out)


def draw_queries(key, part):
    return query_key_pair(key)[0].astype(jnp.bfloat16)


def draw_key_states(key, part):
    return query_key_pair(key)[1].astype(jnp.bfloat16)


def neighbour_table(key):
    base_key = jax.random.fold_in(key, 11)
    draw_one, draw_two = jax.random.split(base_key, 2)
    patch_ids = jnp.arange(NPATCH, dtype=jnp.int32)[None, :, None]
    steps_away = jnp.concatenate([jnp.arange(-REACH, 0, dtype=jnp.int32), jnp.arange(1, REACH + 1, dtype=jnp.int32)])
    targets = patch_ids + steps_away[None, None, :]
    inside = (targets >= 0) & (targets < NPATCH)
    ranking = jax.random.randint(draw_one, (SAMPLES, NPATCH, 2 * REACH), 0, 4096, dtype=jnp.int32) * 16
    ranking = ranking + jnp.arange(2 * REACH, dtype=jnp.int32)[None, None, :] + jnp.where(inside, 0, 1 << 20).astype(jnp.int32)
    ranked_order = jnp.argsort(ranking, axis=-1)
    picked = jnp.take_along_axis(jnp.broadcast_to(targets, ranking.shape), ranked_order, axis=-1)[:, :, :NB]
    capacity = jnp.minimum(jnp.sum(inside.astype(jnp.int32), axis=-1), NB)
    raw_count = jax.random.randint(draw_two, (SAMPLES, NPATCH), 0, 1 << 16, dtype=jnp.int32) % capacity + 1
    middle = (jnp.arange(NPATCH) == NPATCH // 2)[None, :]
    live_count = jnp.where(middle, NB, raw_count).astype(jnp.int32)
    slot_ids = jnp.arange(NB, dtype=jnp.int32)
    neighbour_ids = jnp.where(slot_ids[None, None, :] < live_count[:, :, None], picked, patch_ids)
    return (neighbour_ids.astype(jnp.int32), live_count)


def draw_neighbours(key, part):
    return neighbour_table(key)[0]


def draw_counts(key, part):
    return neighbour_table(key)[1]


def steps_of(stream_key, dims, pieces, low, largest):
    def one(dim, blocks):
        draws = jax.random.uniform(jax.random.fold_in(jax.random.fold_in(stream_key, 6), dim), (blocks,), jnp.float32, low / len(pieces), largest / len(pieces))
        return jnp.repeat(jnp.exp(draws), dims[dim] // blocks).reshape((-1,) + (1,) * (len(dims) - dim - 1))

    loudness = one(*pieces[0])
    for cut in pieces[1:]:
        loudness = loudness * one(*cut)
    return loudness


def noise(key, dims, scale, most, cuts=(), kind=jnp.bfloat16):
    entries = jax.random.normal(key, dims, jnp.float32) * scale
    if len(cuts) > 0:
        entries = steps_of(key, dims, cuts, -0.22, 0.18) * entries
    return jnp.clip(entries, min=-most, max=most).astype(kind)


def setup_inputs(seed: int = 0) -> dict:
    arg_keys = jax.random.split(jax.random.key(seed), 8)
    return {
        "queries": draw_queries(jax.random.fold_in(arg_keys[7], 71), 0),
        "key_states": draw_key_states(jax.random.fold_in(arg_keys[7], 71), 0),
        "values": noise(arg_keys[2], (SAMPLES, SEQLEN, HW), 1.0, 6.0, ((0, 16), (1, 32))),
        "w_out": noise(arg_keys[3], (HW, DW), HW ** -0.5, 0.1875),
        "cotangent": noise(arg_keys[4], (SAMPLES, SEQLEN, DW), 1.0, 6.0, ((0, 16), (1, 32))),
        "neighbours": draw_neighbours(jax.random.fold_in(arg_keys[7], 71), 0),
        "counts": draw_counts(jax.random.fold_in(arg_keys[7], 71), 0),
    }


def to_low(array):
    return lax.optimization_barrier(array.astype(jnp.bfloat16)).astype(jnp.float32)

def patch_terms(query_rows, key_window, value_window, allowed, w_out, cot_rows):
    score_scale = 1.0 / math.sqrt(HD)
    high = lax.Precision.HIGHEST
    query_heads = query_rows.astype(jnp.float32).reshape(PATCH, HEADS, HD)
    key_heads = key_window.astype(jnp.float32).reshape(-1, HEADS, HD)
    value_heads = value_window.astype(jnp.float32).reshape(-1, HEADS, HD)
    scores = jnp.einsum('qhd,khd->hqk', query_heads, key_heads, precision=high) * score_scale
    scores = jnp.where(allowed[None, None, :], scores, -jnp.inf)
    row_max = lax.optimization_barrier(jnp.max(scores, axis=-1, keepdims=True))
    log_total = row_max + jnp.log(lax.optimization_barrier(jnp.sum(jnp.exp(scores - row_max), axis=-1, keepdims=True)))
    attn_probs = jnp.exp(scores - log_total)
    probs_low = to_low(attn_probs)
    attended = jnp.einsum('hqk,khd->qhd', probs_low, value_heads, precision=high)
    attended = attended.reshape(PATCH, HEADS * HD).astype(jnp.bfloat16)
    output = jnp.dot(attended, w_out, preferred_element_type=jnp.float32).astype(jnp.bfloat16)
    grad_attended = jnp.dot(cot_rows, w_out.T, preferred_element_type=jnp.float32).astype(jnp.bfloat16)
    grad_heads = grad_attended.astype(jnp.float32).reshape(PATCH, HEADS, HD)
    attn_heads = attended.astype(jnp.float32).reshape(PATCH, HEADS, HD)
    row_delta = lax.optimization_barrier(jnp.sum(grad_heads * attn_heads, axis=-1)).T[:, :, None]
    grad_probs = jnp.einsum('qhd,khd->hqk', grad_heads, value_heads, precision=high)
    grad_scores = to_low(attn_probs * (grad_probs - row_delta))
    grad_query = jnp.einsum('hqk,khd->qhd', grad_scores, key_heads, precision=high) * score_scale
    grad_query = grad_query.reshape(PATCH, HEADS * HD).astype(jnp.bfloat16)
    key_parts = jnp.einsum('hqk,qhd->khd', grad_scores, query_heads, precision=high) * score_scale
    key_parts = key_parts.reshape(-1, PATCH, HEADS * HD).astype(jnp.bfloat16)
    value_parts = jnp.einsum('hqk,qhd->khd', probs_low, grad_heads, precision=high)
    value_parts = value_parts.reshape(-1, PATCH, HEADS * HD).astype(jnp.bfloat16)
    weight_term = to_low(jnp.dot(attended.T, cot_rows, preferred_element_type=jnp.float32))
    return (output, grad_query, key_parts, value_parts, weight_term)

def collect(parts):
    span = 2 * REACH + 1
    summed = jnp.zeros((NPATCH, PATCH, HEADS * HD), jnp.float32)
    for position in range(span):
        offset = position - REACH
        padded = jnp.pad(parts[:, position].astype(jnp.float32), ((REACH, REACH), (0, 0), (0, 0)))
        summed = summed + padded[REACH - offset:REACH - offset + NPATCH]
    return summed.astype(jnp.bfloat16).reshape(SEQLEN, HEADS * HD)

def reference(queries, key_states, values, w_out, cotangent, neighbours, counts):
    span = 2 * REACH + 1

    def one_sample(inputs):
        query_all, key_all, value_all, cot_all, neighbour_ids, live_counts = inputs
        key_pad = jnp.pad(key_all.reshape(NPATCH, PATCH, HEADS * HD), ((REACH, REACH), (0, 0), (0, 0)))
        value_pad = jnp.pad(value_all.reshape(NPATCH, PATCH, HEADS * HD), ((REACH, REACH), (0, 0), (0, 0)))
        offsets = jnp.arange(-REACH, REACH + 1, dtype=jnp.int32)
        slot_ids = jnp.arange(NB, dtype=jnp.int32)

        def one_patch(patch_id):
            first_row = (patch_id * PATCH).astype(jnp.int32)
            query_rows = lax.dynamic_slice_in_dim(query_all, first_row, PATCH, 0)
            cot_rows = lax.dynamic_slice_in_dim(cot_all, first_row, PATCH, 0)
            key_window = lax.dynamic_slice_in_dim(key_pad, patch_id, span, 0).reshape(span * PATCH, HEADS * HD)
            value_window = lax.dynamic_slice_in_dim(value_pad, patch_id, span, 0).reshape(span * PATCH, HEADS * HD)
            matches = (neighbour_ids[patch_id][None, :] == patch_id + offsets[:, None]) & (slot_ids[None, :] < live_counts[patch_id])
            live_slots = jnp.any(matches, axis=1) | (offsets == 0)
            allowed = jnp.repeat(live_slots, PATCH)
            return patch_terms(query_rows, key_window, value_window, allowed, w_out, cot_rows)
        output, grad_query, key_parts, value_parts, weight_terms = lax.map(one_patch, jnp.arange(NPATCH, dtype=jnp.int32))
        return (output.reshape(SEQLEN, DW), grad_query.reshape(SEQLEN, HEADS * HD), collect(key_parts), collect(value_parts), lax.optimization_barrier(jnp.sum(weight_terms, axis=0)))
    output, grad_queries, grad_keys, grad_values, weight_sums = lax.map(one_sample, (queries, key_states, values, cotangent, neighbours, counts))
    grad_w_out = lax.optimization_barrier(jnp.sum(weight_sums, axis=0))
    return (output, grad_queries, grad_keys, grad_values, grad_w_out)
```

```python
import functools
import math

import jax
import jax.numpy as jnp
from jax import lax
from jax.experimental import pallas as pl
from jax.experimental.pallas import tpu as pltpu
from jax.sharding import PartitionSpec as P

HD = 128
PAIRS = 4
PW = 2 * HD
BF = jnp.bfloat16
F32 = jnp.float32
NX, NY, NZ = 4, 8, 8
MESH = pl.DeviceIdType.MESH


def dot(a, b, ca, cb):
    return lax.dot_general(a, b, (((ca,), (cb,)), ((), ())), preferred_element_type=F32)


def kernel(
    nbr, cnt, q_h, k_h, v_h, w_h, c_h,
    out_h, dq_h, dk_h, dv_h, gw_h,
    q, kv, w, cot, do, att, dq, kvp, kvr, asend, aall, zs, zr, ys, yr, outv, gkv, gw,
    lq, lkv, lw, lc, lo,
    hs, hr, cs, cr, as_, ar, ps, pr_, zss, zrs, yss, yrs,
):
    s = lax.axis_index("seq")
    d = lax.axis_index("dp")
    z_hi, y = s // NY, s % NY
    z_lo, xc = d // 8, d % 8
    x, core = xc // 2, xc % 2
    z = z_hi * 2 + z_lo
    right, left = (s + 1) % 32, (s + 31) % 32

    def dev(ss, dd):
        return {"seq": ss, "dp": dd}

    def grp(j):
        return dev(s, z_lo * 8 + j)

    def zdev(zz):
        return dev((zz // 2) * NY + y, (zz % 2) * 8 + xc)

    def ydev(yy):
        return dev(z_hi * NY + yy, d)

    loads = {}

    def load(key, src, dst, sem):
        c = pltpu.make_async_copy(src, dst, sem)
        c.start()
        loads[key] = c

    for i in range(PAIRS):
        cols = pl.ds(i * PW, PW)
        load(("k", i), k_h.at[0, :, cols], kv.at[i, 0, pl.ds(128, 128), :], lkv.at[i, 0])
        load(("v", i), v_h.at[0, :, cols], kv.at[i, 1, pl.ds(128, 128), :], lkv.at[i, 1])
    load("c", c_h.at[0], cot.at[xc], lc)
    for i in range(PAIRS):
        load(("w", i), w_h.at[pl.ds(i * PW, PW), :], w.at[i], lw.at[i])
        load(("q", i), q_h.at[0, :, pl.ds(i * PW, PW)], q.at[i], lq.at[i])

    barrier = pltpu.get_barrier_semaphore()
    peers = [dev(right, d), dev(left, d)]
    peers += [grp((xc + k) % 8) for k in range(1, 8)]
    peers += [zdev((z + k) % NZ) for k in range(1, NZ)]
    peers += [ydev((y + k) % NY) for k in range(1, NY)]
    for peer in peers:
        pl.semaphore_signal(barrier, inc=1, device_id=peer, device_id_type=MESH)
    pl.semaphore_wait(barrier, len(peers))

    sends = []

    def remote(src, dst, ss, rs, to):
        return pltpu.make_async_remote_copy(
            src_ref=src, dst_ref=dst, send_sem=ss, recv_sem=rs, device_id=to, device_id_type=MESH
        )

    def send(*args):
        c = remote(*args)
        c.start()
        sends.append(c)

    mid = pl.ds(128, 128)
    lo_rows = pl.ds(0, 128)
    hi_rows = pl.ds(256, 128)
    xr = ((x + 1) % NX) * 2 + core
    xl = ((x + 3) % NX) * 2 + core
    xo = ((x + 2) % NX) * 2 + core
    partner = x * 2 + (1 - core)
    half = (pl.ds(0, 64), pl.ds(64, 64))

    def halo(i, way):
        if way == 0:
            return remote(kv.at[i, :, mid, :], kv.at[i, :, lo_rows, :], hs.at[0, i], hr.at[0, i], dev(right, d))
        return remote(kv.at[i, :, mid, :], kv.at[i, :, hi_rows, :], hs.at[1, i], hr.at[1, i], dev(left, d))

    for i in range(PAIRS):
        loads["k", i].wait()
        loads["v", i].wait()
        for way in range(2):
            c = halo(i, way)
            c.start()
            sends.append(c)
        if i == 0:
            loads["c"].wait()
            mine = cot.at[xc]
            for n, (to, first) in enumerate(((xr, 0), (xl, 1))):
                for m, hh in enumerate((first, 1 - first)):
                    send(mine.at[half[hh], :], mine.at[half[hh], :], cs.at[n, m], cr.at[n, m], grp(to))
            send(mine, mine, cs.at[2, 0], cr.at[2, 0], grp(partner))

    c_own = cot[xc]
    for i in range(PAIRS):
        loads["w", i].wait()
        do[i] = dot(c_own, w[i], 1, 1).astype(BF)
    for i in range(PAIRS):
        loads["q", i].wait()

    n0, n1, live = nbr[0, 0, 0], nbr[0, 0, 1], cnt[0, 0]
    neg = -jnp.inf

    def bias(target):
        hit = ((n0 == target) & (live > 0)) | ((n1 == target) & (live > 1))
        return jnp.where(hit, 0.0, neg).astype(F32)

    b_left, b_right = bias(s - 1), bias(s + 1)
    scale = 1.0 / math.sqrt(HD)

    o_id = lax.broadcasted_iota(jnp.int32, (PW, PW), 0)
    f_id = lax.broadcasted_iota(jnp.int32, (PW, PW), 1)
    f_of = ((o_id >> 1) & 7) * 32 + ((o_id >> 4) & 1) * 16 + ((o_id >> 5) & 7) * 2 + (o_id & 1)
    perm = jnp.where(f_id == f_of, 1.0, 0.0).astype(BF)

    def cot_wait(slot, rows, n, m):
        ref = cot.at[slot] if rows is None else cot.at[slot].at[half[rows], :]
        remote(ref, ref, cs.at[n, m], cr.at[n, m], grp(partner)).wait_recv()

    for i in range(PAIRS):
        for way in range(2):
            halo(i, way).wait_recv()
        for h in range(2):
            cols = pl.ds(h * HD, HD)
            qh, doh = q[i, :, cols], do[i, :, cols]
            kh, vh = kv[i, 0, :, cols], kv[i, 1, :, cols]
            t = dot(kh, qh, 1, 1) * scale
            t = jnp.concatenate([t[:128] + b_left, t[128:256], t[256:] + b_right], axis=0)
            e = jnp.exp(t - jnp.max(t, axis=0, keepdims=True))
            p = e * (1.0 / jnp.sum(e, axis=0, keepdims=True))
            pb = p.astype(BF)
            att_h = dot(pb, vh, 0, 0).astype(BF)
            att[:, pl.ds(i * PW + h * HD, HD)] = att_h
            dp = dot(vh, doh, 1, 1)
            delta = jnp.sum(p * dp, axis=0, keepdims=True)
            ds = (p * (dp - delta)).astype(BF)
            dq[i, :, cols] = (dot(ds, kh, 0, 0) * scale).astype(BF)
            kvp[i, 0, :, cols] = (dot(ds, qh, 1, 0) * scale).astype(BF)
            kvp[i, 1, :, cols] = dot(pb, doh, 1, 0).astype(BF)
        a_pair = att[:, pl.ds(i * PW, PW)]
        asend[i] = dot(perm, a_pair, 1, 1).astype(BF).reshape(8, 32, 128)
        rows = pl.ds(i * 32, 32)
        for k in range(1, 8):
            j = (xc + k) % 8
            send(asend.at[i, j], aall.at[xc, rows, :], as_.at[i, k], ar.at[i, k], grp(j))
        aall[xc, rows, :] = asend[i, xc]
        send(kvp.at[i, :, hi_rows, :], kvr.at[0, i], ps.at[0, i], pr_.at[0, i], dev(right, d))
        send(kvp.at[i, :, lo_rows, :], kvr.at[1, i], ps.at[1, i], pr_.at[1, i], dev(left, d))
        if i == 0:
            cot_wait(xl, 0, 0, 0)
            ref = cot.at[xl].at[half[0], :]
            send(ref, ref, cs.at[3, 0], cr.at[3, 0], grp(xr))
            cot_wait(xr, 1, 1, 0)
            ref = cot.at[xr].at[half[1], :]
            send(ref, ref, cs.at[3, 1], cr.at[3, 1], grp(xl))
        if i == 2:
            cot_wait(xl, 1, 0, 1)
            send(cot.at[xl], cot.at[xl], cs.at[4, 0], cr.at[4, 0], grp(partner))
            cot_wait(xr, 0, 1, 1)
            send(cot.at[xr], cot.at[xr], cs.at[4, 1], cr.at[4, 1], grp(partner))
            cot_wait(xo, 0, 3, 0)
            cot_wait(xo, 1, 3, 1)
            send(cot.at[xo], cot.at[xo], cs.at[2, 1], cr.at[2, 1], grp(partner))

    outs = []

    def store(src, dst, sem):
        c = pltpu.make_async_copy(src, dst, sem)
        c.start()
        outs.append(c)

    for i in range(PAIRS):
        store(dq.at[i], dq_h.at[0, :, pl.ds(i * PW, PW)], lo.at[i])
    a_all = att[...]
    outv[...] = sum(dot(a_all[:, i * PW:(i + 1) * PW], w[i], 1, 0) for i in range(PAIRS)).astype(BF)
    store(outv, out_h.at[0], lo.at[4])

    def flip(slot):
        return (slot // 2) * 2 + (1 - slot % 2)

    cot_wait(partner, None, 2, 0)
    cot_wait(flip(xl), None, 4, 0)
    cot_wait(flip(xr), None, 4, 1)
    cot_wait(flip(xo), None, 2, 1)
    for i in range(PAIRS):
        for k in range(1, 8):
            j = (xc + 8 - k) % 8
            ref = aall.at[j, pl.ds(i * 32, 32), :]
            remote(ref, ref, as_.at[i, k], ar.at[i, k], grp(j)).wait_recv()
    a_t = jnp.concatenate([aall[j] for j in range(8)], axis=1)
    zs[...] = dot(a_t, cot[...].reshape(1024, 1024), 1, 0).astype(BF).reshape(NZ, 16, 1024)
    for k in range(1, NZ):
        zz = (z + k) % NZ
        send(zs.at[zz], zr.at[k], zss.at[k], zrs.at[k], zdev(zz))
    total = zs[z].astype(F32)
    for k in range(1, NZ):
        remote(zr.at[k], zr.at[k], zss.at[k], zrs.at[k], zdev((z + NZ - k) % NZ)).wait_recv()
        total = total + zr[k].astype(F32)
    for j in range(NY):
        ys[j] = total[2 * j:2 * j + 2]
    for k in range(1, NY):
        yy = (y + k) % NY
        send(ys.at[yy], yr.at[k], yss.at[k], yrs.at[k], ydev(yy))

    for i in range(PAIRS):
        for way in range(2):
            ref = kvr.at[way, i]
            remote(ref, ref, ps.at[way, i], pr_.at[way, i], dev(left, d)).wait_recv()
        for j in range(2):
            g = kvp[i, j, mid, :].astype(F32) + kvr[0, i, j].astype(F32) + kvr[1, i, j].astype(F32)
            gkv[i, j] = g.astype(BF)
        store(gkv.at[i, 0], dk_h.at[0, :, pl.ds(i * PW, PW)], lo.at[5 + i])
        store(gkv.at[i, 1], dv_h.at[0, :, pl.ds(i * PW, PW)], lo.at[9 + i])

    final = ys[y]
    for k in range(1, NY):
        remote(yr.at[k], yr.at[k], yss.at[k], yrs.at[k], ydev((y + NY - k) % NY)).wait_recv()
        final = final + yr[k]
    gw[...] = final
    store(gw, gw_h, lo.at[13])
    for c in sends:
        c.wait_send()
    for c in outs:
        c.wait()


def on_device(queries, key_states, values, w_out, cotangent, neighbours, counts):
    big = jax.ShapeDtypeStruct((1, 128, 1024), BF)
    any_ = pl.BlockSpec(memory_space=pl.ANY)
    smem = pl.BlockSpec(memory_space=pltpu.SMEM)
    V, D = pltpu.VMEM, pltpu.SemaphoreType.DMA
    return pl.pallas_call(
        kernel,
        name="patch_attention",
        out_shape=(big, big, big, big, jax.ShapeDtypeStruct((2, 1024), F32)),
        in_specs=[smem, smem] + [any_] * 5,
        out_specs=[any_] * 5,
        scratch_shapes=[
            V((4, 128, 256), BF),
            V((4, 2, 384, 256), BF),
            V((4, 256, 1024), BF),
            V((8, 128, 1024), BF),
            V((4, 128, 256), BF),
            V((128, 1024), BF),
            V((4, 128, 256), BF),
            V((4, 2, 384, 256), BF),
            V((2, 4, 2, 128, 256), BF),
            V((4, 8, 32, 128), BF),
            V((8, 128, 128), BF),
            V((8, 16, 1024), BF),
            V((8, 16, 1024), BF),
            V((8, 2, 1024), F32),
            V((8, 2, 1024), F32),
            V((128, 1024), BF),
            V((4, 2, 128, 256), BF),
            V((2, 1024), F32),
            D((4,)), D((4, 2)), D((4,)), D, D((14,)),
            D((2, 4)), D((2, 4)), D((5, 2)), D((5, 2)), D((4, 8)), D((4, 8)),
            D((2, 4)), D((2, 4)), D((8,)), D((8,)), D((8,)), D((8,)),
        ],
        compiler_params=pltpu.CompilerParams(
            collective_id=0, has_side_effects=True, vmem_limit_bytes=60 * 1024 * 1024
        ),
    )(neighbours, counts, queries, key_states, values, w_out, cotangent)


def solution(mesh):
    placed = (
        P("dp", "seq", None),
        P("dp", "seq", None),
        P("dp", "seq", None),
        P(),
        P("dp", "seq", None),
        P("dp", "seq", None),
        P("dp", "seq"),
    )
    return jax.shard_map(
        on_device,
        mesh=mesh,
        in_specs=placed,
        out_specs=(
            P("dp", "seq", None),
            P("dp", "seq", None),
            P("dp", "seq", None),
            P("dp", "seq", None),
            P(("seq", "dp"), None),
        ),
        check_vma=False,
    )
```

```python
import math

import jax
import jax.numpy as jnp
from jax import lax
from jax.experimental import pallas as pl
from jax.experimental.pallas import tpu as pltpu
from jax.sharding import PartitionSpec as P

HD = 128
PAIRS = 4
PW = 2 * HD
BF = jnp.bfloat16
F32 = jnp.float32
NX, NY, NZ = 4, 8, 8
MESH = pl.DeviceIdType.MESH


def dot(a, b, ca, cb):
    return lax.dot_general(a, b, (((ca,), (cb,)), ((), ())), preferred_element_type=F32)


def kernel(
    nbr, cnt, q_h, k_h, v_h, w_h, c_h,
    out_r, dq_r, dk_r, dv_r, gw_r,
    q, kv, w, cot, do, att, kvp, kvr, asend, aall, zs, zr, ys, yr, rb, rb2,
    lq, lkv, lw, lc,
    hs, hr, cs, cr, as_, ar, ps, pr_, zss, zrs, yss, yrs, fs, fr, gs, gr,
):
    s = lax.axis_index("seq")
    d = lax.axis_index("dp")
    z_hi, y = s // NY, s % NY
    z_lo, xc = d // 8, d % 8
    x, core = xc // 2, xc % 2
    z = z_hi * 2 + z_lo

    def grp(j):
        return {"seq": s, "dp": z_lo * 8 + j}

    def zyd(zz, yy):
        return {"seq": (zz // 2) * NY + yy, "dp": (zz % 2) * 8 + xc}

    up, down = (z + 1) % NZ, (z + NZ - 1) % NZ
    yu, yd = (y + 1) % NY, (y + NY - 1) % NY

    barrier = pltpu.get_barrier_semaphore()
    peers = [zyd(up, yu), zyd(down, yd)]
    peers += [grp((xc + k) % 8) for k in range(1, 8)]
    peers += [zyd((z + k) % NZ, y) for k in range(1, NZ)]
    peers += [zyd(z, (y + k) % NY) for k in range(1, NY)]
    for peer in peers:
        pl.semaphore_signal(barrier, inc=1, device_id=peer, device_id_type=MESH)

    loads = {}

    def load(key, src, dst, sem):
        c = pltpu.make_async_copy(src, dst, sem)
        c.start()
        loads[key] = c

    load("c", c_h.at[0], cot.at[xc], lc)
    for i in range(PAIRS):
        load(("w", i), w_h.at[pl.ds(i * PW, PW), :], w.at[i], lw.at[i])
    for i in range(PAIRS):
        cols = pl.ds(i * PW, PW)
        load(("q", i), q_h.at[0, :, cols], q.at[i], lq.at[i])
        load(("k", i), k_h.at[0, :, cols], kv.at[i, 0, pl.ds(128, 128), :], lkv.at[i, 0])
        load(("v", i), v_h.at[0, :, cols], kv.at[i, 1, pl.ds(128, 128), :], lkv.at[i, 1])

    pl.semaphore_wait(barrier, len(peers))

    sends = []

    def remote(src, dst, ss, rs, to):
        return pltpu.make_async_remote_copy(
            src_ref=src, dst_ref=dst, send_sem=ss, recv_sem=rs, device_id=to, device_id_type=MESH
        )

    def send(*args):
        c = remote(*args)
        c.start()
        sends.append(c)

    mid = pl.ds(128, 128)
    side = (pl.ds(0, 128), pl.ds(256, 128))
    xr = ((x + 1) % NX) * 2 + core
    xl = ((x + 3) % NX) * 2 + core
    xo = ((x + 2) % NX) * 2 + core
    partner = x * 2 + (1 - core)
    half = (pl.ds(0, 64), pl.ds(64, 64))

    edge = (y == NY - 1, y == 0)
    next_y = (zyd(z, yu), zyd(z, yd))
    next_z = (zyd(up, y), zyd(down, y))
    next_zy = (zyd(up, yu), zyd(down, yd))

    def to_side(src, dst, relay, ss, rs, rrs, way):
        @pl.when(edge[way])
        def _():
            remote(src, relay, ss, rrs, next_z[way]).start()

        @pl.when(jnp.logical_not(edge[way]))
        def _():
            remote(src, dst, ss, rs, next_y[way]).start()

        sends.append(remote(src, dst, ss, rs, next_y[way]))

    def pass_on(relay, dsts, fss, rss, rrs):
        for way in range(2):
            @pl.when(edge[way])
            def _():
                remote(relay, relay, fss, rrs, next_z[way]).wait_recv()
                remote(relay, dsts[way], fss, rss[way], next_zy[way]).start()

    srcs = (k_h, v_h)

    def halo(i, j, way):
        to_side(
            srcs[j].at[0, :, pl.ds(i * PW, PW)], kv.at[i, j, side[way], :], rb.at[i, j],
            hs.at[way, j, i], hr.at[way, j, i], fr.at[i, j], way,
        )

    for i in range(PAIRS):
        for j in range(2):
            for way in range(2):
                halo(i, j, way)
        if i == 0:
            for n, (to, first) in enumerate(((xr, 0), (xl, 1))):
                for m, hh in enumerate((first, 1 - first)):
                    send(c_h.at[0, half[hh], :], cot.at[xc, half[hh], :], cs.at[n, m], cr.at[n, m], grp(to))
            send(c_h.at[0], cot.at[xc], cs.at[2, 0], cr.at[2, 0], grp(partner))

    loads["c"].wait()
    c_own = cot[xc]
    for i in range(PAIRS):
        loads["w", i].wait()
        do[i] = dot(c_own, w[i], 1, 1).astype(BF)
    for i in range(PAIRS):
        for key in "qkv":
            loads[key, i].wait()

    n0, n1, live = nbr[0, 0, 0], nbr[0, 0, 1], cnt[0, 0]

    def bias(target):
        hit = ((n0 == target) & (live > 0)) | ((n1 == target) & (live > 1))
        return jnp.where(hit, 0.0, -jnp.inf).astype(F32)

    b_left, b_right = bias(s - 1), bias(s + 1)
    scale = 1.0 / math.sqrt(HD)

    o_id = lax.broadcasted_iota(jnp.int32, (PW, PW), 0)
    f_id = lax.broadcasted_iota(jnp.int32, (PW, PW), 1)
    f_of = ((o_id >> 1) & 7) * 32 + ((o_id >> 4) & 1) * 16 + ((o_id >> 5) & 7) * 2 + (o_id & 1)
    perm = jnp.where(f_id == f_of, 1.0, 0.0).astype(BF)

    def cot_wait(slot, rows, n, m):
        ref = cot.at[slot] if rows is None else cot.at[slot, half[rows], :]
        remote(ref, ref, cs.at[n, m], cr.at[n, m], grp(partner)).wait_recv()

    for i in range(PAIRS):
        for j in range(2):
            pass_on(
                rb.at[i, j], [kv.at[i, j, side[way], :] for way in range(2)],
                fs.at[i, j], [hr.at[way, j, i] for way in range(2)], fr.at[i, j],
            )
        for j in range(2):
            for way in range(2):
                ref = kv.at[i, j, side[way], :]
                remote(ref, ref, hs.at[way, j, i], hr.at[way, j, i], next_y[way]).wait_recv()
        kept = []
        for h in range(2):
            cols = pl.ds(h * HD, HD)
            qh, kh, vh = q[i, :, cols], kv[i, 0, :, cols], kv[i, 1, :, cols]
            t = dot(kh, qh, 1, 1) * scale
            t = jnp.concatenate([t[:128] + b_left, t[128:256], t[256:] + b_right], axis=0)
            e = jnp.exp(t - jnp.max(t, axis=0, keepdims=True))
            p = e * (1.0 / jnp.sum(e, axis=0, keepdims=True))
            pb = p.astype(BF)
            att[:, pl.ds(i * PW + h * HD, HD)] = dot(pb, vh, 0, 0).astype(BF)
            kept.append((p, pb))
        a_pair = att[:, pl.ds(i * PW, PW)]
        asend[i] = dot(perm, a_pair, 1, 1).astype(BF).reshape(8, 32, 128)
        rows = pl.ds(i * 32, 32)
        for k in range(1, 8):
            j = (xc + k) % 8
            send(asend.at[i, j], aall.at[xc, rows, :], as_.at[i, k], ar.at[i, k], grp(j))
        aall[xc, rows, :] = asend[i, xc]
        for h in range(2):
            cols = pl.ds(h * HD, HD)
            qh, doh = q[i, :, cols], do[i, :, cols]
            kh, vh = kv[i, 0, :, cols], kv[i, 1, :, cols]
            p, pb = kept[h]
            dp = dot(vh, doh, 1, 1)
            delta = jnp.sum(p * dp, axis=0, keepdims=True)
            ds = (p * (dp - delta)).astype(BF)
            kvp[i, 0, :, cols] = (dot(ds, qh, 1, 0) * scale).astype(BF)
            kvp[i, 1, :, cols] = dot(pb, doh, 1, 0).astype(BF)
            dq_r[0, :, pl.ds(i * PW + h * HD, HD)] = (dot(ds, kh, 0, 0) * scale).astype(BF)
        for j in range(2):
            for way in range(2):
                to_side(
                    kvp.at[i, j, side[1 - way], :], kvr.at[way, i, j], rb2.at[i, j],
                    ps.at[way, j, i], pr_.at[way, j, i], gr.at[i, j], way,
                )
        if i == 0:
            cot_wait(xl, 0, 0, 0)
            ref = cot.at[xl, half[0], :]
            send(ref, ref, cs.at[3, 0], cr.at[3, 0], grp(xr))
            cot_wait(xr, 1, 1, 0)
            ref = cot.at[xr, half[1], :]
            send(ref, ref, cs.at[3, 1], cr.at[3, 1], grp(xl))
        if i == 2:
            cot_wait(xl, 1, 0, 1)
            send(cot.at[xl], cot.at[xl], cs.at[4, 0], cr.at[4, 0], grp(partner))
            cot_wait(xr, 0, 1, 1)
            send(cot.at[xr], cot.at[xr], cs.at[4, 1], cr.at[4, 1], grp(partner))
            cot_wait(xo, 0, 3, 0)
            cot_wait(xo, 1, 3, 1)
            send(cot.at[xo], cot.at[xo], cs.at[2, 1], cr.at[2, 1], grp(partner))

    def flip(slot):
        return (slot // 2) * 2 + (1 - slot % 2)

    cot_wait(partner, None, 2, 0)
    cot_wait(flip(xl), None, 4, 0)
    cot_wait(flip(xr), None, 4, 1)
    cot_wait(flip(xo), None, 2, 1)
    c_all = cot[...].reshape(1024, 1024)

    def zcopy(zz):
        return remote(zs.at[zz], zr.at[z], zss.at[zz], zrs.at[z], zyd(jnp.int32(zz), y))

    def reduce_rows(first, last):
        for i in range(first, last):
            for k in range(1, 8):
                j = (xc + 8 - k) % 8
                ref = aall.at[j, pl.ds(i * 32, 32), :]
                remote(ref, ref, as_.at[i, k], ar.at[i, k], grp(j)).wait_recv()
        a_t = jnp.concatenate([aall[j, pl.ds(first * 32, (last - first) * 32), :] for j in range(8)], axis=1)
        term = dot(a_t, c_all, 1, 0).astype(BF).reshape((last - first) * 2, 16, 1024)
        zs[pl.ds(first * 2, (last - first) * 2)] = term
        for zz in range(first * 2, last * 2):
            @pl.when(z != zz)
            def _():
                zcopy(zz).start()

    def pass_parts(i):
        for j in range(2):
            pass_on(
                rb2.at[i, j], [kvr.at[way, i, j] for way in range(2)],
                gs.at[i, j], [pr_.at[way, j, i] for way in range(2)], gr.at[i, j],
            )

    reduce_rows(0, 3)
    a_all = att[...]
    out_r[0] = sum(dot(a_all[:, i * PW:(i + 1) * PW], w[i], 1, 0) for i in range(PAIRS)).astype(BF)
    pass_parts(0)
    reduce_rows(3, 4)
    for i in range(1, PAIRS):
        pass_parts(i)
    zr[z] = zs[z]
    for zz in range(NZ):
        @pl.when(z != zz)
        def _():
            remote(zr.at[zz], zr.at[zz], zss.at[zz], zrs.at[zz], zyd(jnp.int32(zz), y)).wait_recv()
    total = sum(zr[zz].astype(F32) for zz in range(NZ))
    for j in range(NY):
        ys[j] = total[2 * j:2 * j + 2]
    for k in range(1, NY):
        yy = (y + k) % NY
        send(ys.at[yy], yr.at[k], yss.at[k], yrs.at[k], zyd(z, yy))

    for i in range(PAIRS):
        for j, ref in enumerate((dk_r, dv_r)):
            for way in range(2):
                got = kvr.at[way, i, j]
                remote(got, got, ps.at[way, j, i], pr_.at[way, j, i], next_y[way]).wait_recv()
            g = kvp[i, j, mid, :].astype(F32) + kvr[0, i, j].astype(F32) + kvr[1, i, j].astype(F32)
            ref[0, :, pl.ds(i * PW, PW)] = g.astype(BF)

    final = ys[y]
    for k in range(1, NY):
        remote(yr.at[k], yr.at[k], yss.at[k], yrs.at[k], zyd(z, (y + NY - k) % NY)).wait_recv()
        final = final + yr[k]
    gw_r[...] = final
    for c in sends:
        c.wait_send()
    for zz in range(NZ):
        @pl.when(z != zz)
        def _():
            zcopy(zz).wait_send()

    @pl.when(edge[0] | edge[1])
    def _():
        for i in range(PAIRS):
            for j in range(2):
                remote(rb.at[i, j], rb.at[i, j], fs.at[i, j], fr.at[i, j], next_y[0]).wait_send()
                remote(rb2.at[i, j], rb2.at[i, j], gs.at[i, j], gr.at[i, j], next_y[0]).wait_send()


def flush(*refs):
    sem = refs[-1]
    copies = [pltpu.make_async_copy(refs[n], refs[5 + n], sem.at[n]) for n in range(5)]
    for c in copies:
        c.start()
    for c in copies:
        c.wait()


def on_device(queries, key_states, values, w_out, cotangent, neighbours, counts):
    big = jax.ShapeDtypeStruct((1, 128, 1024), BF)
    hbm = pl.BlockSpec(memory_space=pltpu.HBM)
    vmem = pl.BlockSpec(memory_space=pltpu.VMEM)
    smem = pl.BlockSpec(memory_space=pltpu.SMEM)
    V, D = pltpu.VMEM, pltpu.SemaphoreType.DMA
    results = pl.pallas_call(
        kernel,
        name="patch_attention",
        out_shape=(V((1, 128, 1024), BF),) * 4 + (V((2, 1024), F32),),
        in_specs=[smem, smem] + [hbm] * 5,
        out_specs=[vmem] * 5,
        scratch_shapes=[
            V((4, 128, 256), BF),
            V((4, 2, 384, 256), BF),
            V((4, 256, 1024), BF),
            V((8, 128, 1024), BF),
            V((4, 128, 256), BF),
            V((128, 1024), BF),
            V((4, 2, 384, 256), BF),
            V((2, 4, 2, 128, 256), BF),
            V((4, 8, 32, 128), BF),
            V((8, 128, 128), BF),
            V((8, 16, 1024), BF),
            V((8, 16, 1024), BF),
            V((8, 2, 1024), F32),
            V((8, 2, 1024), F32),
            V((4, 2, 128, 256), BF),
            V((4, 2, 128, 256), BF),
            D((4,)), D((4, 2)), D((4,)), D,
            D((2, 2, 4)), D((2, 2, 4)), D((5, 2)), D((5, 2)), D((4, 8)), D((4, 8)),
            D((2, 2, 4)), D((2, 2, 4)), D((8,)), D((8,)), D((8,)), D((8,)),
            D((4, 2)), D((4, 2)), D((4, 2)), D((4, 2)),
        ],
        compiler_params=pltpu.CompilerParams(
            collective_id=0, has_side_effects=True, vmem_limit_bytes=65_000_000
        ),
    )(neighbours, counts, queries, key_states, values, w_out, cotangent)
    return pl.pallas_call(
        flush,
        name="flush",
        out_shape=(big, big, big, big, jax.ShapeDtypeStruct((2, 1024), F32)),
        in_specs=[vmem] * 5,
        out_specs=[hbm] * 5,
        scratch_shapes=[D((5,))],
        compiler_params=pltpu.CompilerParams(vmem_limit_bytes=4_000_000),
    )(*results)


def solution(mesh):
    placed = (
        P("dp", "seq", None),
        P("dp", "seq", None),
        P("dp", "seq", None),
        P(),
        P("dp", "seq", None),
        P("dp", "seq", None),
        P("dp", "seq"),
    )
    return jax.shard_map(
        on_device,
        mesh=mesh,
        in_specs=placed,
        out_specs=(
            P("dp", "seq", None),
            P("dp", "seq", None),
            P("dp", "seq", None),
            P("dp", "seq", None),
            P(("seq", "dp"), None),
        ),
        check_vma=False,
    )
```

```python
import math

import jax
import jax.numpy as jnp
from jax import lax
from jax.experimental import pallas as pl
from jax.experimental.pallas import tpu as pltpu
from jax.sharding import PartitionSpec as P

HD = 128
PAIRS = 4
PW = 2 * HD
BF = jnp.bfloat16
F32 = jnp.float32
NX, NY, NZ = 4, 8, 8
MESH = pl.DeviceIdType.MESH


def dot(a, b, ca, cb):
    return lax.dot_general(a, b, (((ca,), (cb,)), ((), ())), preferred_element_type=F32)


def kernel(
    nbr, cnt, q_h, k_h, v_h, w_h, c_h,
    out_r, dq_r, dk_r, dv_r, gw_r,
    q, kv, w, cot, do, att, kvp, kvr, asend, aall, zs, zr, rb, rb2,
    lq, lkv, lw, lc,
    hs, hr, cs, cr, as_, ar, ps, pr_, zss, zrs, fs, fr, gs, gr,
):
    s = lax.axis_index("seq")
    d = lax.axis_index("dp")
    z_hi, y = s // NY, s % NY
    z_lo, xc = d // 8, d % 8
    x, core = xc // 2, xc % 2
    z = z_hi * 2 + z_lo

    def grp(j):
        return {"seq": s, "dp": z_lo * 8 + j}

    def zyd(zz, yy):
        return {"seq": (zz // 2) * NY + yy, "dp": (zz % 2) * 8 + xc}

    up, down = (z + 1) % NZ, (z + NZ - 1) % NZ
    yu, yd = (y + 1) % NY, (y + NY - 1) % NY

    barrier = pltpu.get_barrier_semaphore()
    me = z * NY + y

    def place(c):
        return zyd(c // NY, c % NY)

    def greet(k, carry):
        pl.semaphore_signal(barrier, inc=1, device_id=place((me + k) % 64), device_id_type=MESH)
        return carry

    for k in range(1, 8):
        pl.semaphore_signal(barrier, inc=1, device_id=grp((xc + k) % 8), device_id_type=MESH)
    lax.fori_loop(1, 64, greet, 0)

    loads = {}

    def load(key, src, dst, sem):
        c = pltpu.make_async_copy(src, dst, sem)
        c.start()
        loads[key] = c

    load("c", c_h.at[0], cot.at[xc], lc)
    for i in range(PAIRS):
        load(("w", i), w_h.at[pl.ds(i * PW, PW), :], w.at[i], lw.at[i])
    for i in range(PAIRS):
        cols = pl.ds(i * PW, PW)
        load(("q", i), q_h.at[0, :, cols], q.at[i], lq.at[i])
        load(("k", i), k_h.at[0, :, cols], kv.at[i, 0, pl.ds(128, 128), :], lkv.at[i, 0])
        load(("v", i), v_h.at[0, :, cols], kv.at[i, 1, pl.ds(128, 128), :], lkv.at[i, 1])

    pl.semaphore_wait(barrier, 70)

    sends = []

    def remote(src, dst, ss, rs, to):
        return pltpu.make_async_remote_copy(
            src_ref=src, dst_ref=dst, send_sem=ss, recv_sem=rs, device_id=to, device_id_type=MESH
        )

    def send(*args):
        c = remote(*args)
        c.start()
        sends.append(c)

    mid = pl.ds(128, 128)
    side = (pl.ds(0, 128), pl.ds(256, 128))
    xr = ((x + 1) % NX) * 2 + core
    xl = ((x + 3) % NX) * 2 + core
    xo = ((x + 2) % NX) * 2 + core
    partner = x * 2 + (1 - core)
    half = (pl.ds(0, 64), pl.ds(64, 64))

    edge = (y == NY - 1, y == 0)
    next_y = (zyd(z, yu), zyd(z, yd))
    next_z = (zyd(up, y), zyd(down, y))
    next_zy = (zyd(up, yu), zyd(down, yd))

    def to_side(src, dst, relay, ss, rs, rrs, way):
        @pl.when(edge[way])
        def _():
            remote(src, relay, ss, rrs, next_z[way]).start()

        @pl.when(jnp.logical_not(edge[way]))
        def _():
            remote(src, dst, ss, rs, next_y[way]).start()

        sends.append(remote(src, dst, ss, rs, next_y[way]))

    def pass_on(relay, dsts, fss, rss, rrs):
        for way in range(2):
            @pl.when(edge[way])
            def _():
                remote(relay, relay, fss, rrs, next_z[way]).wait_recv()
                remote(relay, dsts[way], fss, rss[way], next_zy[way]).start()

    srcs = (k_h, v_h)

    def halo(i, j, way):
        to_side(
            srcs[j].at[0, :, pl.ds(i * PW, PW)], kv.at[i, j, side[way], :], rb.at[i, j],
            hs.at[way, j, i], hr.at[way, j, i], fr.at[i, j], way,
        )

    for i in range(PAIRS):
        for j in range(2):
            for way in range(2):
                halo(i, j, way)
        if i == 0:
            for n, (to, first) in enumerate(((xr, 0), (xl, 1))):
                for m, hh in enumerate((first, 1 - first)):
                    send(c_h.at[0, half[hh], :], cot.at[xc, half[hh], :], cs.at[n, m], cr.at[n, m], grp(to))

    send(c_h.at[0], cot.at[xc], cs.at[2, 0], cr.at[2, 0], grp(partner))

    loads["c"].wait()
    c_own = cot[xc]
    for i in range(PAIRS):
        loads["w", i].wait()
        do[i] = dot(c_own, w[i], 1, 1).astype(BF)
    for i in range(PAIRS):
        for key in "qkv":
            loads[key, i].wait()

    n0, n1, live = nbr[0, 0, 0], nbr[0, 0, 1], cnt[0, 0]

    def bias(target):
        hit = ((n0 == target) & (live > 0)) | ((n1 == target) & (live > 1))
        return jnp.where(hit, 0.0, -jnp.inf).astype(F32)

    b_left, b_right = bias(s - 1), bias(s + 1)
    scale = 1.0 / math.sqrt(HD)

    o_id = lax.broadcasted_iota(jnp.int32, (PW, PW), 0)
    f_id = lax.broadcasted_iota(jnp.int32, (PW, PW), 1)
    f_of = ((o_id >> 1) & 7) * 32 + ((o_id >> 4) & 1) * 16 + ((o_id >> 5) & 7) * 2 + (o_id & 1)
    perm = jnp.where(f_id == f_of, 1.0, 0.0).astype(BF)

    def cot_wait(slot, rows, n, m):
        ref = cot.at[slot] if rows is None else cot.at[slot, half[rows], :]
        remote(ref, ref, cs.at[n, m], cr.at[n, m], grp(partner)).wait_recv()

    def pass_halo(i):
        for j in range(2):
            pass_on(
                rb.at[i, j], [kv.at[i, j, side[way], :] for way in range(2)],
                fs.at[i, j], [hr.at[way, j, i] for way in range(2)], fr.at[i, j],
            )

    def flip(slot):
        return (slot // 2) * 2 + (1 - slot % 2)

    def chunk(c):
        return remote(zs.at[c], zr.at[(me + 64 - c) % 64], zss, zrs, place(c))

    def reduce_rows(first, last):
        for i in range(first, last):
            for k in range(1, 8):
                j = (xc + 8 - k) % 8
                ref = aall.at[j, pl.ds(i * 32, 32), :]
                remote(ref, ref, as_.at[i, k], ar.at[i, k], grp(j)).wait_recv()
        a_t = jnp.concatenate([aall[j, pl.ds(first * 32, (last - first) * 32), :] for j in range(8)], axis=1)
        term = dot(a_t, cot[...].reshape(1024, 1024), 1, 0)
        count = (last - first) * 16
        zs[pl.ds(first * 16, count)] = term.reshape(count, 16, 128).astype(BF)

        def hand_out(k, carry):
            c = first * 16 + (me + k) % count

            @pl.when(c != me)
            def _():
                chunk(c).start()

            return carry

        lax.fori_loop(0, count, hand_out, 0)

    def pass_parts(i):
        for j in range(2):
            pass_on(
                rb2.at[i, j], [kvr.at[way, i, j] for way in range(2)],
                gs.at[i, j], [pr_.at[way, j, i] for way in range(2)], gr.at[i, j],
            )

    def return_parts(i):
        for j in range(2):
            for way in range(2):
                to_side(
                    kvp.at[i, j, side[1 - way], :], kvr.at[way, i, j], rb2.at[i, j],
                    ps.at[way, j, i], pr_.at[way, j, i], gr.at[i, j], way,
                )

    pass_halo(0)
    pass_halo(1)
    for i in range(PAIRS):
        if i + 2 < PAIRS:
            pass_halo(i + 2)
        for j in range(2):
            for way in range(2):
                ref = kv.at[i, j, side[way], :]
                remote(ref, ref, hs.at[way, j, i], hr.at[way, j, i], next_y[way]).wait_recv()
        kept = []
        for h in range(2):
            cols = pl.ds(h * HD, HD)
            qh, kh, vh = q[i, :, cols], kv[i, 0, :, cols], kv[i, 1, :, cols]
            t = dot(kh, qh, 1, 1) * scale
            t = jnp.concatenate([t[:128] + b_left, t[128:256], t[256:] + b_right], axis=0)
            e = jnp.exp(t - jnp.max(t, axis=0, keepdims=True))
            p = e * (1.0 / jnp.sum(e, axis=0, keepdims=True))
            pb = p.astype(BF)
            att[:, pl.ds(i * PW + h * HD, HD)] = dot(pb, vh, 0, 0).astype(BF)
            kept.append((p, pb))
        a_pair = att[:, pl.ds(i * PW, PW)]
        asend[i] = dot(perm, a_pair, 1, 1).astype(BF).reshape(8, 32, 128)
        rows = pl.ds(i * 32, 32)
        for k in range(1, 8):
            j = (xc + k) % 8
            send(asend.at[i, j], aall.at[xc, rows, :], as_.at[i, k], ar.at[i, k], grp(j))
        aall[xc, rows, :] = asend[i, xc]
        if i == 2:
            cot_wait(xo, 0, 3, 0)
            cot_wait(xo, 1, 3, 1)
            send(cot.at[xo], cot.at[xo], cs.at[2, 1], cr.at[2, 1], grp(partner))
        for h in range(2):
            cols = pl.ds(h * HD, HD)
            qh, doh = q[i, :, cols], do[i, :, cols]
            kh, vh = kv[i, 0, :, cols], kv[i, 1, :, cols]
            p, pb = kept[h]
            dp = dot(vh, doh, 1, 1)
            delta = jnp.sum(p * dp, axis=0, keepdims=True)
            ds = (p * (dp - delta)).astype(BF)
            kvp[i, 0, :, cols] = (dot(ds, qh, 1, 0) * scale).astype(BF)
            kvp[i, 1, :, cols] = dot(pb, doh, 1, 0).astype(BF)
            dq_r[0, :, pl.ds(i * PW + h * HD, HD)] = (dot(ds, kh, 0, 0) * scale).astype(BF)
        return_parts(i)
        if i == 0:
            cot_wait(xl, 0, 0, 0)
            ref = cot.at[xl, half[0], :]
            send(ref, ref, cs.at[3, 0], cr.at[3, 0], grp(xr))
            cot_wait(xr, 1, 1, 0)
            ref = cot.at[xr, half[1], :]
            send(ref, ref, cs.at[3, 1], cr.at[3, 1], grp(xl))
        if i == 1:
            cot_wait(xl, 1, 0, 1)
            send(cot.at[xl], cot.at[xl], cs.at[4, 0], cr.at[4, 0], grp(partner))
            cot_wait(xr, 0, 1, 1)
            send(cot.at[xr], cot.at[xr], cs.at[4, 1], cr.at[4, 1], grp(partner))

    pass_parts(0)
    cot_wait(partner, None, 2, 0)
    cot_wait(flip(xl), None, 4, 0)
    cot_wait(flip(xr), None, 4, 1)
    cot_wait(flip(xo), None, 2, 1)
    reduce_rows(0, 3)
    a_all = att[...]
    out_r[0] = sum(dot(a_all[:, i * PW:(i + 1) * PW], w[i], 1, 0) for i in range(PAIRS)).astype(BF)
    reduce_rows(3, 4)
    pass_parts(1)
    pass_parts(2)
    pass_parts(3)
    for i in range(PAIRS):
        for j, ref in enumerate((dk_r, dv_r)):
            for way in range(2):
                got = kvr.at[way, i, j]
                remote(got, got, ps.at[way, j, i], pr_.at[way, j, i], next_y[way]).wait_recv()
            g = kvp[i, j, mid, :].astype(F32) + kvr[0, i, j].astype(F32) + kvr[1, i, j].astype(F32)
            ref[0, :, pl.ds(i * PW, PW)] = g.astype(BF)

    everyone = pl.ds(1, 63)
    remote(zs.at[everyone], zr.at[everyone], zss, zrs, next_y[0]).wait_recv()
    final = zs[me].astype(F32) + jnp.sum(zr[everyone].astype(F32), axis=0)
    for j in range(8):
        gw_r[:, pl.ds(j * 128, 128)] = jnp.concatenate([final[j:j + 1], final[8 + j:9 + j]], axis=0)
    for c in sends:
        c.wait_send()
    remote(zs.at[everyone], zr.at[everyone], zss, zrs, next_y[0]).wait_send()

    @pl.when(edge[0] | edge[1])
    def _():
        for i in range(PAIRS):
            for j in range(2):
                remote(rb.at[i, j], rb.at[i, j], fs.at[i, j], fr.at[i, j], next_y[0]).wait_send()
                remote(rb2.at[i, j], rb2.at[i, j], gs.at[i, j], gr.at[i, j], next_y[0]).wait_send()


def flush(*refs):
    sem = refs[-1]
    copies = [pltpu.make_async_copy(refs[n], refs[5 + n], sem.at[n]) for n in range(5)]
    for c in copies:
        c.start()
    for c in copies:
        c.wait()


def on_device(queries, key_states, values, w_out, cotangent, neighbours, counts):
    big = jax.ShapeDtypeStruct((1, 128, 1024), BF)
    hbm = pl.BlockSpec(memory_space=pltpu.HBM)
    vmem = pl.BlockSpec(memory_space=pltpu.VMEM)
    smem = pl.BlockSpec(memory_space=pltpu.SMEM)
    V, D = pltpu.VMEM, pltpu.SemaphoreType.DMA
    results = pl.pallas_call(
        kernel,
        name="patch_attention",
        out_shape=(V((1, 128, 1024), BF),) * 4 + (V((2, 1024), F32),),
        in_specs=[smem, smem] + [hbm] * 5,
        out_specs=[vmem] * 5,
        scratch_shapes=[
            V((4, 128, 256), BF),
            V((4, 2, 384, 256), BF),
            V((4, 256, 1024), BF),
            V((8, 128, 1024), BF),
            V((4, 128, 256), BF),
            V((128, 1024), BF),
            V((4, 2, 384, 256), BF),
            V((2, 4, 2, 128, 256), BF),
            V((4, 8, 32, 128), BF),
            V((8, 128, 128), BF),
            V((64, 16, 128), BF),
            V((64, 16, 128), BF),
            V((4, 2, 128, 256), BF),
            V((4, 2, 128, 256), BF),
            D((4,)), D((4, 2)), D((4,)), D,
            D((2, 2, 4)), D((2, 2, 4)), D((5, 2)), D((5, 2)), D((4, 8)), D((4, 8)),
            D((2, 2, 4)), D((2, 2, 4)), D, D,
            D((4, 2)), D((4, 2)), D((4, 2)), D((4, 2)),
        ],
        compiler_params=pltpu.CompilerParams(
            collective_id=0, has_side_effects=True, vmem_limit_bytes=65_000_000
        ),
    )(neighbours, counts, queries, key_states, values, w_out, cotangent)
    return pl.pallas_call(
        flush,
        name="flush",
        out_shape=(big, big, big, big, jax.ShapeDtypeStruct((2, 1024), F32)),
        in_specs=[vmem] * 5,
        out_specs=[hbm] * 5,
        scratch_shapes=[D((5,))],
        compiler_params=pltpu.CompilerParams(vmem_limit_bytes=4_000_000),
    )(*results)


def solution(mesh):
    placed = (
        P("dp", "seq", None),
        P("dp", "seq", None),
        P("dp", "seq", None),
        P(),
        P("dp", "seq", None),
        P("dp", "seq", None),
        P("dp", "seq"),
    )
    return jax.shard_map(
        on_device,
        mesh=mesh,
        in_specs=placed,
        out_specs=(
            P("dp", "seq", None),
            P("dp", "seq", None),
            P("dp", "seq", None),
            P("dp", "seq", None),
            P(("seq", "dp"), None),
        ),
        check_vma=False,
    )
```

```python
import math

import jax
import jax.numpy as jnp
from jax import lax
from jax.experimental import pallas as pl
from jax.experimental.pallas import tpu as pltpu
from jax.sharding import PartitionSpec as P

HD = 128
PAIRS = 4
PW = 2 * HD
BF = jnp.bfloat16
F32 = jnp.float32
NX, NY, NZ = 4, 8, 8
MESH = pl.DeviceIdType.MESH


def dot(a, b, ca, cb):
    return lax.dot_general(a, b, (((ca,), (cb,)), ((), ())), preferred_element_type=F32)


def kernel(
    nbr_h, cnt, q_h, k_h, v_h, w_h, c_h,
    out_r, dq_r, dk_r, dv_r, gw_r,
    q, kv, w, cot, do, att, kvp, kvr, asend, aall, zs, zr, rb, rb2,
    lq, lkv, lw, lc,
    hs, hr, cs, cr, as_, ar, ps, pr_, zss, zrs, fs, fr, gs, gr, far, nbr, ln,
):
    s = lax.axis_index("seq")
    d = lax.axis_index("dp")
    z_hi, y = s // NY, s % NY
    z_lo, xc = d // 8, d % 8
    x, core = xc // 2, xc % 2
    z = z_hi * 2 + z_lo

    def grp(j):
        return {"seq": s, "dp": z_lo * 8 + j}

    def zyd(zz, yy):
        return {"seq": (zz // 2) * NY + yy, "dp": (zz % 2) * 8 + xc}

    up, down = (z + 1) % NZ, (z + NZ - 1) % NZ
    yu, yd = (y + 1) % NY, (y + NY - 1) % NY

    barrier = pltpu.get_barrier_semaphore()
    me = z * NY + y

    def place(c):
        return zyd(c // NY, c % NY)

    peers = [zyd(up, yu), zyd(down, yd)]
    peers += [grp((xc + k) % 8) for k in range(1, 8)]
    peers += [zyd((z + k) % NZ, y) for k in range(1, NZ)]
    peers += [zyd(z, (y + k) % NY) for k in range(1, NY)]
    for peer in peers:
        pl.semaphore_signal(barrier, inc=1, device_id=peer, device_id_type=MESH)

    loads = {}

    def load(key, src, dst, sem):
        c = pltpu.make_async_copy(src, dst, sem)
        c.start()
        loads[key] = c

    load("n", nbr_h, nbr, ln)
    load("c", c_h.at[0], cot.at[xc], lc)
    for i in range(PAIRS):
        load(("w", i), w_h.at[pl.ds(i * PW, PW), :], w.at[i], lw.at[i])
    for i in range(PAIRS):
        cols = pl.ds(i * PW, PW)
        load(("q", i), q_h.at[0, :, cols], q.at[i], lq.at[i])
        load(("k", i), k_h.at[0, :, cols], kv.at[i, 0, pl.ds(128, 128), :], lkv.at[i, 0])
        load(("v", i), v_h.at[0, :, cols], kv.at[i, 1, pl.ds(128, 128), :], lkv.at[i, 1])

    pl.semaphore_wait(barrier, len(peers))

    sends = []

    def remote(src, dst, ss, rs, to):
        return pltpu.make_async_remote_copy(
            src_ref=src, dst_ref=dst, send_sem=ss, recv_sem=rs, device_id=to, device_id_type=MESH
        )

    def send(*args):
        c = remote(*args)
        c.start()
        sends.append(c)

    mid = pl.ds(128, 128)
    side = (pl.ds(0, 128), pl.ds(256, 128))
    xr = ((x + 1) % NX) * 2 + core
    xl = ((x + 3) % NX) * 2 + core
    xo = ((x + 2) % NX) * 2 + core
    partner = x * 2 + (1 - core)
    half = (pl.ds(0, 64), pl.ds(64, 64))

    edge = (y == NY - 1, y == 0)
    next_y = (zyd(z, yu), zyd(z, yd))
    next_z = (zyd(up, y), zyd(down, y))
    next_zy = (zyd(up, yu), zyd(down, yd))

    def to_side(src, dst, relay, ss, rs, rrs, way):
        @pl.when(edge[way])
        def _():
            remote(src, relay, ss, rrs, next_z[way]).start()

        @pl.when(jnp.logical_not(edge[way]))
        def _():
            remote(src, dst, ss, rs, next_y[way]).start()

        sends.append(remote(src, dst, ss, rs, next_y[way]))

    def pass_on(relay, dsts, fss, rss, rrs):
        for way in range(2):
            @pl.when(edge[way])
            def _():
                remote(relay, relay, fss, rrs, next_z[way]).wait_recv()
                remote(relay, dsts[way], fss, rss[way], next_zy[way]).start()

    srcs = (k_h, v_h)

    def halo(i, j, way):
        to_side(
            srcs[j].at[0, :, pl.ds(i * PW, PW)], kv.at[i, j, side[way], :], rb.at[i, j],
            hs.at[way, j, i], hr.at[way, j, i], fr.at[i, j], way,
        )

    for i in range(PAIRS):
        for j in range(2):
            for way in range(2):
                halo(i, j, way)
        if i == 0:
            for n, (to, first) in enumerate(((xr, 0), (xl, 1))):
                for m, hh in enumerate((first, 1 - first)):
                    send(c_h.at[0, half[hh], :], cot.at[xc, half[hh], :], cs.at[n, m], cr.at[n, m], grp(to))

    send(c_h.at[0], cot.at[xc], cs.at[2, 0], cr.at[2, 0], grp(partner))

    for k in range(1, NY):
        pl.semaphore_signal(far, inc=1, device_id=zyd(z, (y + k) % NY), device_id_type=MESH)

    loads["c"].wait()
    c_own = cot[xc]
    for i in range(PAIRS):
        loads["w", i].wait()
        do[i] = dot(c_own, w[i], 1, 1).astype(BF)
    for i in range(PAIRS):
        for key in "qkv":
            loads[key, i].wait()

    loads["n"].wait()
    n0, n1, live = nbr[0, 0, 0], nbr[0, 0, 1], cnt[0, 0]

    def bias(target):
        hit = ((n0 == target) & (live > 0)) | ((n1 == target) & (live > 1))
        return jnp.where(hit, 0.0, -jnp.inf).astype(F32)

    b_left, b_right = bias(s - 1), bias(s + 1)
    scale = 1.0 / math.sqrt(HD)

    o_id = lax.broadcasted_iota(jnp.int32, (PW, PW), 0)
    f_id = lax.broadcasted_iota(jnp.int32, (PW, PW), 1)
    f_of = ((o_id >> 1) & 7) * 32 + ((o_id >> 4) & 1) * 16 + ((o_id >> 5) & 7) * 2 + (o_id & 1)
    perm = jnp.where(f_id == f_of, 1.0, 0.0).astype(BF)

    def cot_wait(slot, rows, n, m):
        ref = cot.at[slot] if rows is None else cot.at[slot, half[rows], :]
        remote(ref, ref, cs.at[n, m], cr.at[n, m], grp(partner)).wait_recv()

    def pass_halo(i):
        for j in range(2):
            pass_on(
                rb.at[i, j], [kv.at[i, j, side[way], :] for way in range(2)],
                fs.at[i, j], [hr.at[way, j, i] for way in range(2)], fr.at[i, j],
            )

    def flip(slot):
        return (slot // 2) * 2 + (1 - slot % 2)

    def chunk(c):
        return remote(zs.at[c], zr.at[(me + 64 - c) % 64], zss, zrs, place(c))

    def reduce_rows(first, last):
        for i in range(first, last):
            for k in range(1, 8):
                j = (xc + 8 - k) % 8
                ref = aall.at[j, pl.ds(i * 32, 32), :]
                remote(ref, ref, as_.at[i, k], ar.at[i, k], grp(j)).wait_recv()
        a_t = jnp.concatenate([aall[j, pl.ds(first * 32, (last - first) * 32), :] for j in range(8)], axis=1)
        term = dot(a_t, cot[...].reshape(1024, 1024), 1, 0)
        count = (last - first) * 16
        zs[pl.ds(first * 16, count)] = term.reshape(count, 16, 128).astype(BF)

        def hand_out(k, carry):
            c = first * 16 + (me + k) % count

            @pl.when(c != me)
            def _():
                chunk(c).start()

            return carry

        lax.fori_loop(0, count, hand_out, 0)

    def pass_parts(i):
        for j in range(2):
            pass_on(
                rb2.at[i, j], [kvr.at[way, i, j] for way in range(2)],
                gs.at[i, j], [pr_.at[way, j, i] for way in range(2)], gr.at[i, j],
            )

    def return_parts(i):
        for j in range(2):
            for way in range(2):
                to_side(
                    kvp.at[i, j, side[1 - way], :], kvr.at[way, i, j], rb2.at[i, j],
                    ps.at[way, j, i], pr_.at[way, j, i], gr.at[i, j], way,
                )

    pass_halo(0)
    pass_halo(1)
    for i in range(PAIRS):
        if i + 2 < PAIRS:
            pass_halo(i + 2)
        for j in range(2):
            for way in range(2):
                ref = kv.at[i, j, side[way], :]
                remote(ref, ref, hs.at[way, j, i], hr.at[way, j, i], next_y[way]).wait_recv()
        kept = []
        for h in range(2):
            cols = pl.ds(h * HD, HD)
            qh, kh, vh = q[i, :, cols], kv[i, 0, :, cols], kv[i, 1, :, cols]
            t = dot(kh, qh, 1, 1) * scale
            t = jnp.concatenate([t[:128] + b_left, t[128:256], t[256:] + b_right], axis=0)
            e = jnp.exp(t - jnp.max(t, axis=0, keepdims=True))
            p = e * (1.0 / jnp.sum(e, axis=0, keepdims=True))
            pb = p.astype(BF)
            att[:, pl.ds(i * PW + h * HD, HD)] = dot(pb, vh, 0, 0).astype(BF)
            kept.append((p, pb))
        a_pair = att[:, pl.ds(i * PW, PW)]
        asend[i] = dot(perm, a_pair, 1, 1).astype(BF).reshape(8, 32, 128)
        rows = pl.ds(i * 32, 32)
        for k in range(1, 8):
            j = (xc + k) % 8
            send(asend.at[i, j], aall.at[xc, rows, :], as_.at[i, k], ar.at[i, k], grp(j))
        aall[xc, rows, :] = asend[i, xc]
        if i == 2:
            cot_wait(xo, 0, 3, 0)
            cot_wait(xo, 1, 3, 1)
            send(cot.at[xo], cot.at[xo], cs.at[2, 1], cr.at[2, 1], grp(partner))
        if i == 3:
            pass_parts(0)
        for h in range(2):
            cols = pl.ds(h * HD, HD)
            qh, doh = q[i, :, cols], do[i, :, cols]
            kh, vh = kv[i, 0, :, cols], kv[i, 1, :, cols]
            p, pb = kept[h]
            dp = dot(vh, doh, 1, 1)
            delta = jnp.sum(p * dp, axis=0, keepdims=True)
            ds = (p * (dp - delta)).astype(BF)
            kvp[i, 0, :, cols] = (dot(ds, qh, 1, 0) * scale).astype(BF)
            kvp[i, 1, :, cols] = dot(pb, doh, 1, 0).astype(BF)
            dq_r[0, :, pl.ds(i * PW + h * HD, HD)] = (dot(ds, kh, 0, 0) * scale).astype(BF)
        return_parts(i)
        if i == 0:
            cot_wait(xl, 0, 0, 0)
            ref = cot.at[xl, half[0], :]
            send(ref, ref, cs.at[3, 0], cr.at[3, 0], grp(xr))
            cot_wait(xr, 1, 1, 0)
            ref = cot.at[xr, half[1], :]
            send(ref, ref, cs.at[3, 1], cr.at[3, 1], grp(xl))
        if i == 1:
            cot_wait(xl, 1, 0, 1)
            send(cot.at[xl], cot.at[xl], cs.at[4, 0], cr.at[4, 0], grp(partner))
            cot_wait(xr, 0, 1, 1)
            send(cot.at[xr], cot.at[xr], cs.at[4, 1], cr.at[4, 1], grp(partner))

    pass_parts(1)
    a_all = att[...]
    out_r[0] = sum(dot(a_all[:, i * PW:(i + 1) * PW], w[i], 1, 0) for i in range(PAIRS)).astype(BF)
    pass_parts(2)
    cot_wait(partner, None, 2, 0)
    cot_wait(flip(xl), None, 4, 0)
    cot_wait(flip(xr), None, 4, 1)
    cot_wait(flip(xo), None, 2, 1)
    pl.semaphore_wait(far, NY - 1)
    reduce_rows(0, 4)
    pass_parts(3)

    for i in range(PAIRS):
        for j, ref in enumerate((dk_r, dv_r)):
            for way in range(2):
                got = kvr.at[way, i, j]
                remote(got, got, ps.at[way, j, i], pr_.at[way, j, i], next_y[way]).wait_recv()
            g = kvp[i, j, mid, :].astype(F32) + kvr[0, i, j].astype(F32) + kvr[1, i, j].astype(F32)
            ref[0, :, pl.ds(i * PW, PW)] = g.astype(BF)

    everyone = pl.ds(1, 63)
    remote(zs.at[everyone], zr.at[everyone], zss, zrs, next_y[0]).wait_recv()
    final = zs[me].astype(F32) + jnp.sum(zr[everyone].astype(F32), axis=0)
    for j in range(8):
        gw_r[:, pl.ds(j * 128, 128)] = jnp.concatenate([final[j:j + 1], final[8 + j:9 + j]], axis=0)
    for c in sends:
        c.wait_send()
    remote(zs.at[everyone], zr.at[everyone], zss, zrs, next_y[0]).wait_send()

    @pl.when(edge[0] | edge[1])
    def _():
        for i in range(PAIRS):
            for j in range(2):
                remote(rb.at[i, j], rb.at[i, j], fs.at[i, j], fr.at[i, j], next_y[0]).wait_send()
                remote(rb2.at[i, j], rb2.at[i, j], gs.at[i, j], gr.at[i, j], next_y[0]).wait_send()


def flush(*refs):
    sem = refs[-1]
    copies = [pltpu.make_async_copy(refs[n], refs[5 + n], sem.at[n]) for n in range(5)]
    for c in copies:
        c.start()
    for c in copies:
        c.wait()


def on_device(queries, key_states, values, w_out, cotangent, neighbours, counts):
    big = jax.ShapeDtypeStruct((1, 128, 1024), BF)
    hbm = pl.BlockSpec(memory_space=pltpu.HBM)
    vmem = pl.BlockSpec(memory_space=pltpu.VMEM)
    smem = pl.BlockSpec(memory_space=pltpu.SMEM)
    V, D = pltpu.VMEM, pltpu.SemaphoreType.DMA
    results = pl.pallas_call(
        kernel,
        name="patch_attention",
        out_shape=(V((1, 128, 1024), BF),) * 4 + (V((2, 1024), F32),),
        in_specs=[hbm, smem] + [hbm] * 5,
        out_specs=[vmem] * 5,
        scratch_shapes=[
            V((4, 128, 256), BF),
            V((4, 2, 384, 256), BF),
            V((4, 256, 1024), BF),
            V((8, 128, 1024), BF),
            V((4, 128, 256), BF),
            V((128, 1024), BF),
            V((4, 2, 384, 256), BF),
            V((2, 4, 2, 128, 256), BF),
            V((4, 8, 32, 128), BF),
            V((8, 128, 128), BF),
            V((64, 16, 128), BF),
            V((64, 16, 128), BF),
            V((4, 2, 128, 256), BF),
            V((4, 2, 128, 256), BF),
            D((4,)), D((4, 2)), D((4,)), D,
            D((2, 2, 4)), D((2, 2, 4)), D((5, 2)), D((5, 2)), D((4, 8)), D((4, 8)),
            D((2, 2, 4)), D((2, 2, 4)), D, D,
            D((4, 2)), D((4, 2)), D((4, 2)), D((4, 2)), pltpu.SemaphoreType.REGULAR,
            pltpu.SMEM((1, 1, 2), jnp.int32), D,
        ],
        compiler_params=pltpu.CompilerParams(
            collective_id=0, has_side_effects=True, vmem_limit_bytes=65_000_000
        ),
    )(neighbours, counts, queries, key_states, values, w_out, cotangent)
    return pl.pallas_call(
        flush,
        name="flush",
        out_shape=(big, big, big, big, jax.ShapeDtypeStruct((2, 1024), F32)),
        in_specs=[vmem] * 5,
        out_specs=[hbm] * 5,
        scratch_shapes=[D((5,))],
        compiler_params=pltpu.CompilerParams(vmem_limit_bytes=4_000_000),
    )(*results)


def solution(mesh):
    placed = (
        P("dp", "seq", None),
        P("dp", "seq", None),
        P("dp", "seq", None),
        P(),
        P("dp", "seq", None),
        P("dp", "seq", None),
        P("dp", "seq"),
    )
    return jax.shard_map(
        on_device,
        mesh=mesh,
        in_specs=placed,
        out_specs=(
            P("dp", "seq", None),
            P("dp", "seq", None),
            P("dp", "seq", None),
            P("dp", "seq", None),
            P(("seq", "dp"), None),
        ),
        check_vma=False,
    )
```

```python
import math

import jax
import jax.numpy as jnp
from jax import lax
from jax.experimental import pallas as pl
from jax.experimental.pallas import tpu as pltpu
from jax.sharding import PartitionSpec as P

HD = 128
PAIRS = 4
PW = 2 * HD
BF = jnp.bfloat16
F32 = jnp.float32
NX, NY, NZ = 4, 8, 8
MESH = pl.DeviceIdType.MESH


def dot(a, b, ca, cb):
    return lax.dot_general(a, b, (((ca,), (cb,)), ((), ())), preferred_element_type=F32)


def kernel(
    nbr_h, cnt, q_h, k_h, v_h, w_h, c_h,
    out_r, dq_r, dk_r, dv_r, gw_r,
    q, kv, w, cot, do, att, kvp, kvr, asend, aall, zs, zr, rb, rb2,
    lq, lkv, lw, lc,
    hs, hr, cs, cr, as_, ar, ps, pr_, zss, zrs, fs, fr, gs, gr, far, nbr, ln,
):
    s = lax.axis_index("seq")
    d = lax.axis_index("dp")
    z_hi, y = s // NY, s % NY
    z_lo, xc = d // 8, d % 8
    x, core = xc // 2, xc % 2
    z = z_hi * 2 + z_lo

    def grp(j):
        return {"seq": s, "dp": z_lo * 8 + j}

    def zyd(zz, yy):
        return {"seq": (zz // 2) * NY + yy, "dp": (zz % 2) * 8 + xc}

    up, down = (z + 1) % NZ, (z + NZ - 1) % NZ
    yu, yd = (y + 1) % NY, (y + NY - 1) % NY

    barrier = pltpu.get_barrier_semaphore()
    me = z * NY + y

    def place(c):
        return zyd(c // NY, c % NY)

    peers = [zyd(up, yu), zyd(down, yd)]
    peers += [grp((xc + k) % 8) for k in range(1, 8)]
    peers += [zyd((z + k) % NZ, y) for k in range(1, NZ)]
    peers += [zyd(z, (y + k) % NY) for k in range(1, NY)]
    for peer in peers:
        pl.semaphore_signal(barrier, inc=1, device_id=peer, device_id_type=MESH)

    loads = {}

    def load(key, src, dst, sem):
        c = pltpu.make_async_copy(src, dst, sem)
        c.start()
        loads[key] = c

    load("n", nbr_h, nbr, ln)
    load("c", c_h.at[0], cot.at[xc], lc)
    for i in range(PAIRS):
        load(("w", i), w_h.at[pl.ds(i * PW, PW), :], w.at[i], lw.at[i])
    for i in range(PAIRS):
        cols = pl.ds(i * PW, PW)
        load(("q", i), q_h.at[0, :, cols], q.at[i], lq.at[i])
        load(("k", i), k_h.at[0, :, cols], kv.at[i, 0, pl.ds(128, 128), :], lkv.at[i, 0])
        load(("v", i), v_h.at[0, :, cols], kv.at[i, 1, pl.ds(128, 128), :], lkv.at[i, 1])

    pl.semaphore_wait(barrier, len(peers))

    sends = []

    def remote(src, dst, ss, rs, to):
        return pltpu.make_async_remote_copy(
            src_ref=src, dst_ref=dst, send_sem=ss, recv_sem=rs, device_id=to, device_id_type=MESH
        )

    def send(*args):
        c = remote(*args)
        c.start()
        sends.append(c)

    mid = pl.ds(128, 128)
    side = (pl.ds(0, 128), pl.ds(256, 128))
    xr = ((x + 1) % NX) * 2 + core
    xl = ((x + 3) % NX) * 2 + core
    xo = ((x + 2) % NX) * 2 + core
    partner = x * 2 + (1 - core)
    half = (pl.ds(0, 64), pl.ds(64, 64))

    edge = (y == NY - 1, y == 0)
    next_y = (zyd(z, yu), zyd(z, yd))
    next_z = (zyd(up, y), zyd(down, y))
    next_zy = (zyd(up, yu), zyd(down, yd))

    def to_side(src, dst, relay, ss, rs, rrs, way):
        @pl.when(edge[way])
        def _():
            remote(src, relay, ss, rrs, next_z[way]).start()

        @pl.when(jnp.logical_not(edge[way]))
        def _():
            remote(src, dst, ss, rs, next_y[way]).start()

        sends.append(remote(src, dst, ss, rs, next_y[way]))

    def pass_on(relay, dsts, fss, rss, rrs):
        for way in range(2):
            @pl.when(edge[way])
            def _():
                remote(relay, relay, fss, rrs, next_z[way]).wait_recv()
                remote(relay, dsts[way], fss, rss[way], next_zy[way]).start()

    srcs = (k_h, v_h)

    def halo(i, j, way):
        to_side(
            srcs[j].at[0, :, pl.ds(i * PW, PW)], kv.at[i, j, side[way], :], rb.at[i, j],
            hs.at[way, j, i], hr.at[way, j, i], fr.at[i, j], way,
        )

    for i in range(PAIRS):
        for j in range(2):
            for way in range(2):
                halo(i, j, way)
        if i == 0:
            for n, (to, first) in enumerate(((xr, 0), (xl, 1))):
                for m, hh in enumerate((first, 1 - first)):
                    send(c_h.at[0, half[hh], :], cot.at[xc, half[hh], :], cs.at[n, m], cr.at[n, m], grp(to))

    send(c_h.at[0], cot.at[xc], cs.at[2, 0], cr.at[2, 0], grp(partner))

    for k in range(1, NY):
        pl.semaphore_signal(far, inc=1, device_id=zyd(z, (y + k) % NY), device_id_type=MESH)

    loads["c"].wait()
    c_own = cot[xc]
    for i in range(PAIRS):
        loads["w", i].wait()
        do[i] = dot(c_own, w[i], 1, 1).astype(BF)
    for i in range(PAIRS):
        for key in "qkv":
            loads[key, i].wait()

    loads["n"].wait()
    n0, n1, live = nbr[0, 0, 0], nbr[0, 0, 1], cnt[0, 0]

    def bias(target):
        hit = ((n0 == target) & (live > 0)) | ((n1 == target) & (live > 1))
        return jnp.where(hit, 0.0, -jnp.inf).astype(F32)

    b_left, b_right = bias(s - 1), bias(s + 1)
    scale = 1.0 / math.sqrt(HD)

    o_id = lax.broadcasted_iota(jnp.int32, (PW, PW), 0)
    f_id = lax.broadcasted_iota(jnp.int32, (PW, PW), 1)
    f_of = ((o_id >> 1) & 7) * 32 + ((o_id >> 4) & 1) * 16 + ((o_id >> 5) & 7) * 2 + (o_id & 1)
    perm = jnp.where(f_id == f_of, 1.0, 0.0).astype(BF)

    def cot_wait(slot, rows, n, m):
        ref = cot.at[slot] if rows is None else cot.at[slot, half[rows], :]
        remote(ref, ref, cs.at[n, m], cr.at[n, m], grp(partner)).wait_recv()

    def pass_halo(i):
        for j in range(2):
            pass_on(
                rb.at[i, j], [kv.at[i, j, side[way], :] for way in range(2)],
                fs.at[i, j], [hr.at[way, j, i] for way in range(2)], fr.at[i, j],
            )

    def flip(slot):
        return (slot // 2) * 2 + (1 - slot % 2)

    def chunk(c):
        return remote(zs.at[c], zr.at[(me + 64 - c) % 64], zss, zrs, place(c))

    def reduce_rows(first, last):
        for i in range(first, last):
            for k in range(1, 8):
                j = (xc + 8 - k) % 8
                ref = aall.at[j, pl.ds(i * 32, 32), :]
                remote(ref, ref, as_.at[i, k], ar.at[i, k], grp(j)).wait_recv()
        a_t = jnp.concatenate([aall[j, pl.ds(first * 32, (last - first) * 32), :] for j in range(8)], axis=1)
        term = dot(a_t, cot[...].reshape(1024, 1024), 1, 0)
        count = (last - first) * 16
        zs[pl.ds(first * 16, count)] = term.reshape(count, 16, 128).astype(BF)

        def hand_out(k, carry):
            c = first * 16 + (me + k) % count

            @pl.when(c != me)
            def _():
                chunk(c).start()

            return carry

        lax.fori_loop(0, count, hand_out, 0)

    def pass_parts(i):
        for j in range(2):
            pass_on(
                rb2.at[i, j], [kvr.at[way, i, j] for way in range(2)],
                gs.at[i, j], [pr_.at[way, j, i] for way in range(2)], gr.at[i, j],
            )

    def return_parts(i):
        for j in range(2):
            for way in range(2):
                to_side(
                    kvp.at[i, j, side[1 - way], :], kvr.at[way, i, j], rb2.at[i, j],
                    ps.at[way, j, i], pr_.at[way, j, i], gr.at[i, j], way,
                )

    pass_halo(0)
    pass_halo(1)
    for i in range(PAIRS):
        if i + 2 < PAIRS:
            pass_halo(i + 2)
        for j in range(2):
            for way in range(2):
                ref = kv.at[i, j, side[way], :]
                remote(ref, ref, hs.at[way, j, i], hr.at[way, j, i], next_y[way]).wait_recv()
        kept = []
        for h in range(2):
            cols = pl.ds(h * HD, HD)
            qh, kh, vh = q[i, :, cols], kv[i, 0, :, cols], kv[i, 1, :, cols]
            t = dot(kh, qh, 1, 1) * scale
            t = jnp.concatenate([t[:128] + b_left, t[128:256], t[256:] + b_right], axis=0)
            e = jnp.exp(t - jnp.max(t, axis=0, keepdims=True))
            p = e * (1.0 / jnp.sum(e, axis=0, keepdims=True))
            pb = p.astype(BF)
            att[:, pl.ds(i * PW + h * HD, HD)] = dot(pb, vh, 0, 0).astype(BF)
            kept.append((p, pb))
        a_pair = att[:, pl.ds(i * PW, PW)]
        asend[i] = dot(perm, a_pair, 1, 1).astype(BF).reshape(8, 32, 128)
        rows = pl.ds(i * 32, 32)
        for k in range(1, 8):
            j = (xc + k) % 8
            send(asend.at[i, j], aall.at[xc, rows, :], as_.at[i, k], ar.at[i, k], grp(j))
        aall[xc, rows, :] = asend[i, xc]
        if i == 2:
            cot_wait(xo, 0, 3, 0)
            cot_wait(xo, 1, 3, 1)
            send(cot.at[xo], cot.at[xo], cs.at[2, 1], cr.at[2, 1], grp(partner))
        if i == 3:
            pass_parts(0)
        for h in range(2):
            cols = pl.ds(h * HD, HD)
            qh, doh = q[i, :, cols], do[i, :, cols]
            kh, vh = kv[i, 0, :, cols], kv[i, 1, :, cols]
            p, pb = kept[h]
            dp = dot(vh, doh, 1, 1)
            delta = jnp.sum(p * dp, axis=0, keepdims=True)
            ds = (p * (dp - delta)).astype(BF)
            kvp[i, 0, :, cols] = (dot(ds, qh, 1, 0) * scale).astype(BF)
            kvp[i, 1, :, cols] = dot(pb, doh, 1, 0).astype(BF)
            dq_r[0, :, pl.ds(i * PW + h * HD, HD)] = (dot(ds, kh, 0, 0) * scale).astype(BF)
        return_parts(i)
        if i == 0:
            cot_wait(xl, 0, 0, 0)
            ref = cot.at[xl, half[0], :]
            send(ref, ref, cs.at[3, 0], cr.at[3, 0], grp(xr))
            cot_wait(xr, 1, 1, 0)
            ref = cot.at[xr, half[1], :]
            send(ref, ref, cs.at[3, 1], cr.at[3, 1], grp(xl))
        if i == 1:
            cot_wait(xl, 1, 0, 1)
            send(cot.at[xl], cot.at[xl], cs.at[4, 0], cr.at[4, 0], grp(partner))
            cot_wait(xr, 0, 1, 1)
            send(cot.at[xr], cot.at[xr], cs.at[4, 1], cr.at[4, 1], grp(partner))

    pass_parts(1)
    pass_parts(2)
    cot_wait(partner, None, 2, 0)
    cot_wait(flip(xl), None, 4, 0)
    cot_wait(flip(xr), None, 4, 1)
    cot_wait(flip(xo), None, 2, 1)
    pl.semaphore_wait(far, NY - 1)
    reduce_rows(0, 4)
    a_all = att[...]
    out_r[0] = sum(dot(a_all[:, i * PW:(i + 1) * PW], w[i], 1, 0) for i in range(PAIRS)).astype(BF)
    pass_parts(3)

    for i in range(PAIRS):
        for j, ref in enumerate((dk_r, dv_r)):
            for way in range(2):
                got = kvr.at[way, i, j]
                remote(got, got, ps.at[way, j, i], pr_.at[way, j, i], next_y[way]).wait_recv()
            g = kvp[i, j, mid, :].astype(F32) + kvr[0, i, j].astype(F32) + kvr[1, i, j].astype(F32)
            ref[0, :, pl.ds(i * PW, PW)] = g.astype(BF)

    everyone = pl.ds(1, 63)
    remote(zs.at[everyone], zr.at[everyone], zss, zrs, next_y[0]).wait_recv()
    final = zs[me].astype(F32) + jnp.sum(zr[everyone].astype(F32), axis=0)
    for j in range(8):
        gw_r[:, pl.ds(j * 128, 128)] = jnp.concatenate([final[j:j + 1], final[8 + j:9 + j]], axis=0)
    for c in sends:
        c.wait_send()
    remote(zs.at[everyone], zr.at[everyone], zss, zrs, next_y[0]).wait_send()

    @pl.when(edge[0] | edge[1])
    def _():
        for i in range(PAIRS):
            for j in range(2):
                remote(rb.at[i, j], rb.at[i, j], fs.at[i, j], fr.at[i, j], next_y[0]).wait_send()
                remote(rb2.at[i, j], rb2.at[i, j], gs.at[i, j], gr.at[i, j], next_y[0]).wait_send()


def flush(*refs):
    sem = refs[-1]
    copies = [pltpu.make_async_copy(refs[n], refs[5 + n], sem.at[n]) for n in range(5)]
    for c in copies:
        c.start()
    for c in copies:
        c.wait()


def on_device(queries, key_states, values, w_out, cotangent, neighbours, counts):
    big = jax.ShapeDtypeStruct((1, 128, 1024), BF)
    hbm = pl.BlockSpec(memory_space=pltpu.HBM)
    vmem = pl.BlockSpec(memory_space=pltpu.VMEM)
    smem = pl.BlockSpec(memory_space=pltpu.SMEM)
    V, D = pltpu.VMEM, pltpu.SemaphoreType.DMA
    results = pl.pallas_call(
        kernel,
        name="patch_attention",
        out_shape=(V((1, 128, 1024), BF),) * 4 + (V((2, 1024), F32),),
        in_specs=[hbm, smem] + [hbm] * 5,
        out_specs=[vmem] * 5,
        scratch_shapes=[
            V((4, 128, 256), BF),
            V((4, 2, 384, 256), BF),
            V((4, 256, 1024), BF),
            V((8, 128, 1024), BF),
            V((4, 128, 256), BF),
            V((128, 1024), BF),
            V((4, 2, 384, 256), BF),
            V((2, 4, 2, 128, 256), BF),
            V((4, 8, 32, 128), BF),
            V((8, 128, 128), BF),
            V((64, 16, 128), BF),
            V((64, 16, 128), BF),
            V((4, 2, 128, 256), BF),
            V((4, 2, 128, 256), BF),
            D((4,)), D((4, 2)), D((4,)), D,
            D((2, 2, 4)), D((2, 2, 4)), D((5, 2)), D((5, 2)), D((4, 8)), D((4, 8)),
            D((2, 2, 4)), D((2, 2, 4)), D, D,
            D((4, 2)), D((4, 2)), D((4, 2)), D((4, 2)), pltpu.SemaphoreType.REGULAR,
            pltpu.SMEM((1, 1, 2), jnp.int32), D,
        ],
        compiler_params=pltpu.CompilerParams(
            collective_id=0, has_side_effects=True, vmem_limit_bytes=65_000_000
        ),
    )(neighbours, counts, queries, key_states, values, w_out, cotangent)
    return pl.pallas_call(
        flush,
        name="flush",
        out_shape=(big, big, big, big, jax.ShapeDtypeStruct((2, 1024), F32)),
        in_specs=[vmem] * 5,
        out_specs=[hbm] * 5,
        scratch_shapes=[D((5,))],
        compiler_params=pltpu.CompilerParams(vmem_limit_bytes=4_000_000),
    )(*results)


def solution(mesh):
    placed = (
        P("dp", "seq", None),
        P("dp", "seq", None),
        P("dp", "seq", None),
        P(),
        P("dp", "seq", None),
        P("dp", "seq", None),
        P("dp", "seq"),
    )
    return jax.shard_map(
        on_device,
        mesh=mesh,
        in_specs=placed,
        out_specs=(
            P("dp", "seq", None),
            P("dp", "seq", None),
            P("dp", "seq", None),
            P("dp", "seq", None),
            P(("seq", "dp"), None),
        ),
        check_vma=False,
    )
```

```python
import math

import jax
import jax.numpy as jnp
from jax import lax
from jax.experimental import pallas as pl
from jax.experimental.pallas import tpu as pltpu
from jax.sharding import PartitionSpec as P

HD = 128
PAIRS = 4
PW = 2 * HD
BF = jnp.bfloat16
F32 = jnp.float32
NX, NY, NZ = 4, 8, 8
MESH = pl.DeviceIdType.MESH


def dot(a, b, ca, cb):
    return lax.dot_general(a, b, (((ca,), (cb,)), ((), ())), preferred_element_type=F32)


def kernel(
    nbr_h, cnt, q_h, k_h, v_h, w_h, c_h,
    out_r, dq_r, dk_r, dv_r, gw_r,
    q, kv, w, cot, do, att, kvp, kvr, asend, aall, zs, zr, rb, rb2,
    lq, lkv, lw, lc,
    hs, hr, cs, cr, as_, ar, ps, pr_, zss, zrs, fs, fr, gs, gr, far, nbr, ln,
):
    s = lax.axis_index("seq")
    d = lax.axis_index("dp")
    z_hi, y = s // NY, s % NY
    z_lo, xc = d // 8, d % 8
    x, core = xc // 2, xc % 2
    z = z_hi * 2 + z_lo

    def grp(j):
        return {"seq": s, "dp": z_lo * 8 + j}

    def zyd(zz, yy):
        return {"seq": (zz // 2) * NY + yy, "dp": (zz % 2) * 8 + xc}

    up, down = (z + 1) % NZ, (z + NZ - 1) % NZ
    yu, yd = (y + 1) % NY, (y + NY - 1) % NY

    barrier = pltpu.get_barrier_semaphore()
    me = z * NY + y

    def place(c):
        return zyd(c // NY, c % NY)

    peers = [zyd(up, yu), zyd(down, yd)]
    peers += [grp((xc + k) % 8) for k in range(1, 8)]
    peers += [zyd((z + k) % NZ, y) for k in range(1, NZ)]
    peers += [zyd(z, (y + k) % NY) for k in range(1, NY)]
    for peer in peers:
        pl.semaphore_signal(barrier, inc=1, device_id=peer, device_id_type=MESH)

    loads = {}

    def load(key, src, dst, sem):
        c = pltpu.make_async_copy(src, dst, sem)
        c.start()
        loads[key] = c

    load("n", nbr_h, nbr, ln)
    load("c", c_h.at[0], cot.at[xc], lc)
    for i in range(PAIRS):
        load(("w", i), w_h.at[pl.ds(i * PW, PW), :], w.at[i], lw.at[i])
    for i in range(PAIRS):
        cols = pl.ds(i * PW, PW)
        load(("q", i), q_h.at[0, :, cols], q.at[i], lq.at[i])
        load(("k", i), k_h.at[0, :, cols], kv.at[i, 0, pl.ds(128, 128), :], lkv.at[i, 0])
        load(("v", i), v_h.at[0, :, cols], kv.at[i, 1, pl.ds(128, 128), :], lkv.at[i, 1])

    pl.semaphore_wait(barrier, len(peers))

    sends = []

    def remote(src, dst, ss, rs, to):
        return pltpu.make_async_remote_copy(
            src_ref=src, dst_ref=dst, send_sem=ss, recv_sem=rs, device_id=to, device_id_type=MESH
        )

    def send(*args):
        c = remote(*args)
        c.start()
        sends.append(c)

    mid = pl.ds(128, 128)
    side = (pl.ds(0, 128), pl.ds(256, 128))
    xr = ((x + 1) % NX) * 2 + core
    xl = ((x + 3) % NX) * 2 + core
    xo = ((x + 2) % NX) * 2 + core
    partner = x * 2 + (1 - core)
    half = (pl.ds(0, 64), pl.ds(64, 64))

    edge = (y == NY - 1, y == 0)
    next_y = (zyd(z, yu), zyd(z, yd))
    next_z = (zyd(up, y), zyd(down, y))
    next_zy = (zyd(up, yu), zyd(down, yd))

    def to_side(src, dst, relay, ss, rs, rrs, way):
        @pl.when(edge[way])
        def _():
            remote(src, relay, ss, rrs, next_z[way]).start()

        @pl.when(jnp.logical_not(edge[way]))
        def _():
            remote(src, dst, ss, rs, next_y[way]).start()

        sends.append(remote(src, dst, ss, rs, next_y[way]))

    def pass_on(relay, dsts, fss, rss, rrs):
        for way in range(2):
            @pl.when(edge[way])
            def _():
                remote(relay, relay, fss, rrs, next_z[way]).wait_recv()
                remote(relay, dsts[way], fss, rss[way], next_zy[way]).start()

    srcs = (k_h, v_h)

    def halo(i, j, way):
        to_side(
            srcs[j].at[0, :, pl.ds(i * PW, PW)], kv.at[i, j, side[way], :], rb.at[i, j],
            hs.at[way, j, i], hr.at[way, j, i], fr.at[i, j], way,
        )

    for i in range(PAIRS):
        for j in range(2):
            for way in range(2):
                halo(i, j, way)
        if i == 0:
            for n, (to, first) in enumerate(((xr, 0), (xl, 1))):
                for m, hh in enumerate((first, 1 - first)):
                    send(c_h.at[0, half[hh], :], cot.at[xc, half[hh], :], cs.at[n, m], cr.at[n, m], grp(to))

    send(c_h.at[0], cot.at[xc], cs.at[2, 0], cr.at[2, 0], grp(partner))

    for k in range(1, NY):
        pl.semaphore_signal(far, inc=1, device_id=zyd(z, (y + k) % NY), device_id_type=MESH)

    loads["c"].wait()
    c_own = cot[xc]
    for i in range(PAIRS):
        loads["w", i].wait()
        do[i] = dot(c_own, w[i], 1, 1).astype(BF)
    for i in range(PAIRS):
        for key in "qkv":
            loads[key, i].wait()

    loads["n"].wait()
    n0, n1, live = nbr[0, 0, 0], nbr[0, 0, 1], cnt[0, 0]

    def bias(target):
        hit = ((n0 == target) & (live > 0)) | ((n1 == target) & (live > 1))
        return jnp.where(hit, 0.0, -jnp.inf).astype(F32)

    b_left, b_right = bias(s - 1), bias(s + 1)
    scale = 1.0 / math.sqrt(HD)

    o_id = lax.broadcasted_iota(jnp.int32, (PW, PW), 0)
    f_id = lax.broadcasted_iota(jnp.int32, (PW, PW), 1)
    f_of = ((o_id >> 1) & 7) * 32 + ((o_id >> 4) & 1) * 16 + ((o_id >> 5) & 7) * 2 + (o_id & 1)
    perm = jnp.where(f_id == f_of, 1.0, 0.0).astype(BF)

    def cot_wait(slot, rows, n, m):
        ref = cot.at[slot] if rows is None else cot.at[slot, half[rows], :]
        remote(ref, ref, cs.at[n, m], cr.at[n, m], grp(partner)).wait_recv()

    def pass_halo(i):
        for j in range(2):
            pass_on(
                rb.at[i, j], [kv.at[i, j, side[way], :] for way in range(2)],
                fs.at[i, j], [hr.at[way, j, i] for way in range(2)], fr.at[i, j],
            )

    def flip(slot):
        return (slot // 2) * 2 + (1 - slot % 2)

    def chunk(c):
        return remote(zs.at[c], zr.at[(me + 64 - c) % 64], zss, zrs, place(c))

    def reduce_rows(first, last):
        for i in range(first, last):
            for k in range(1, 8):
                j = (xc + 8 - k) % 8
                ref = aall.at[j, pl.ds(i * 32, 32), :]
                remote(ref, ref, as_.at[i, k], ar.at[i, k], grp(j)).wait_recv()
        a_t = jnp.concatenate([aall[j, pl.ds(first * 32, (last - first) * 32), :] for j in range(8)], axis=1)
        term = dot(a_t, cot[...].reshape(1024, 1024), 1, 0)
        count = (last - first) * 16
        zs[pl.ds(first * 16, count)] = term.reshape(count, 16, 128).astype(BF)

        def hand_out(k, carry):
            t = k // NY
            dz = 4 + ((t + 1) // 2) * (1 - 2 * (t % 2))
            c = ((z + dz) % NZ) * NY + (y + 4 + k) % NY

            @pl.when(c != me)
            def _():
                chunk(c).start()

            return carry

        lax.fori_loop(0, count, hand_out, 0)

    def pass_parts(i):
        for j in range(2):
            pass_on(
                rb2.at[i, j], [kvr.at[way, i, j] for way in range(2)],
                gs.at[i, j], [pr_.at[way, j, i] for way in range(2)], gr.at[i, j],
            )

    def return_parts(i):
        for j in range(2):
            for way in range(2):
                to_side(
                    kvp.at[i, j, side[1 - way], :], kvr.at[way, i, j], rb2.at[i, j],
                    ps.at[way, j, i], pr_.at[way, j, i], gr.at[i, j], way,
                )

    pass_halo(0)
    pass_halo(1)
    for i in range(PAIRS):
        if i + 2 < PAIRS:
            pass_halo(i + 2)
        for j in range(2):
            for way in range(2):
                ref = kv.at[i, j, side[way], :]
                remote(ref, ref, hs.at[way, j, i], hr.at[way, j, i], next_y[way]).wait_recv()
        kept = []
        for h in range(2):
            cols = pl.ds(h * HD, HD)
            qh, kh, vh = q[i, :, cols], kv[i, 0, :, cols], kv[i, 1, :, cols]
            t = dot(kh, qh, 1, 1) * scale
            t = jnp.concatenate([t[:128] + b_left, t[128:256], t[256:] + b_right], axis=0)
            e = jnp.exp(t - jnp.max(t, axis=0, keepdims=True))
            p = e * (1.0 / jnp.sum(e, axis=0, keepdims=True))
            pb = p.astype(BF)
            att[:, pl.ds(i * PW + h * HD, HD)] = dot(pb, vh, 0, 0).astype(BF)
            kept.append((p, pb))
        a_pair = att[:, pl.ds(i * PW, PW)]
        asend[i] = dot(perm, a_pair, 1, 1).astype(BF).reshape(8, 32, 128)
        rows = pl.ds(i * 32, 32)
        for k in range(1, 8):
            j = (xc + k) % 8
            send(asend.at[i, j], aall.at[xc, rows, :], as_.at[i, k], ar.at[i, k], grp(j))
        aall[xc, rows, :] = asend[i, xc]
        if i == 2:
            cot_wait(xo, 0, 3, 0)
            cot_wait(xo, 1, 3, 1)
            send(cot.at[xo], cot.at[xo], cs.at[2, 1], cr.at[2, 1], grp(partner))
        if i == 3:
            pass_parts(0)
        for h in range(2):
            cols = pl.ds(h * HD, HD)
            qh, doh = q[i, :, cols], do[i, :, cols]
            kh, vh = kv[i, 0, :, cols], kv[i, 1, :, cols]
            p, pb = kept[h]
            dp = dot(vh, doh, 1, 1)
            delta = jnp.sum(p * dp, axis=0, keepdims=True)
            ds = (p * (dp - delta)).astype(BF)
            kvp[i, 0, :, cols] = (dot(ds, qh, 1, 0) * scale).astype(BF)
            kvp[i, 1, :, cols] = dot(pb, doh, 1, 0).astype(BF)
            dq_r[0, :, pl.ds(i * PW + h * HD, HD)] = (dot(ds, kh, 0, 0) * scale).astype(BF)
        return_parts(i)
        if i == 0:
            cot_wait(xl, 0, 0, 0)
            ref = cot.at[xl, half[0], :]
            send(ref, ref, cs.at[3, 0], cr.at[3, 0], grp(xr))
            cot_wait(xr, 1, 1, 0)
            ref = cot.at[xr, half[1], :]
            send(ref, ref, cs.at[3, 1], cr.at[3, 1], grp(xl))
        if i == 1:
            cot_wait(xl, 1, 0, 1)
            send(cot.at[xl], cot.at[xl], cs.at[4, 0], cr.at[4, 0], grp(partner))
            cot_wait(xr, 0, 1, 1)
            send(cot.at[xr], cot.at[xr], cs.at[4, 1], cr.at[4, 1], grp(partner))

    pass_parts(1)
    pass_parts(2)
    cot_wait(partner, None, 2, 0)
    cot_wait(flip(xl), None, 4, 0)
    cot_wait(flip(xr), None, 4, 1)
    cot_wait(flip(xo), None, 2, 1)
    pl.semaphore_wait(far, NY - 1)
    reduce_rows(0, 4)
    a_all = att[...]
    out_r[0] = sum(dot(a_all[:, i * PW:(i + 1) * PW], w[i], 1, 0) for i in range(PAIRS)).astype(BF)
    pass_parts(3)

    for i in range(PAIRS):
        for j, ref in enumerate((dk_r, dv_r)):
            for way in range(2):
                got = kvr.at[way, i, j]
                remote(got, got, ps.at[way, j, i], pr_.at[way, j, i], next_y[way]).wait_recv()
            g = kvp[i, j, mid, :].astype(F32) + kvr[0, i, j].astype(F32) + kvr[1, i, j].astype(F32)
            ref[0, :, pl.ds(i * PW, PW)] = g.astype(BF)

    everyone = pl.ds(1, 63)
    remote(zs.at[everyone], zr.at[everyone], zss, zrs, next_y[0]).wait_recv()
    final = zs[me].astype(F32) + jnp.sum(zr[everyone].astype(F32), axis=0)
    for j in range(8):
        gw_r[:, pl.ds(j * 128, 128)] = jnp.concatenate([final[j:j + 1], final[8 + j:9 + j]], axis=0)
    for c in sends:
        c.wait_send()
    remote(zs.at[everyone], zr.at[everyone], zss, zrs, next_y[0]).wait_send()

    @pl.when(edge[0] | edge[1])
    def _():
        for i in range(PAIRS):
            for j in range(2):
                remote(rb.at[i, j], rb.at[i, j], fs.at[i, j], fr.at[i, j], next_y[0]).wait_send()
                remote(rb2.at[i, j], rb2.at[i, j], gs.at[i, j], gr.at[i, j], next_y[0]).wait_send()


def flush(*refs):
    sem = refs[-1]
    copies = [pltpu.make_async_copy(refs[n], refs[5 + n], sem.at[n]) for n in range(5)]
    for c in copies:
        c.start()
    for c in copies:
        c.wait()


def on_device(queries, key_states, values, w_out, cotangent, neighbours, counts):
    big = jax.ShapeDtypeStruct((1, 128, 1024), BF)
    hbm = pl.BlockSpec(memory_space=pltpu.HBM)
    vmem = pl.BlockSpec(memory_space=pltpu.VMEM)
    smem = pl.BlockSpec(memory_space=pltpu.SMEM)
    V, D = pltpu.VMEM, pltpu.SemaphoreType.DMA
    results = pl.pallas_call(
        kernel,
        name="patch_attention",
        out_shape=(V((1, 128, 1024), BF),) * 4 + (V((2, 1024), F32),),
        in_specs=[hbm, smem] + [hbm] * 5,
        out_specs=[vmem] * 5,
        scratch_shapes=[
            V((4, 128, 256), BF),
            V((4, 2, 384, 256), BF),
            V((4, 256, 1024), BF),
            V((8, 128, 1024), BF),
            V((4, 128, 256), BF),
            V((128, 1024), BF),
            V((4, 2, 384, 256), BF),
            V((2, 4, 2, 128, 256), BF),
            V((4, 8, 32, 128), BF),
            V((8, 128, 128), BF),
            V((64, 16, 128), BF),
            V((64, 16, 128), BF),
            V((4, 2, 128, 256), BF),
            V((4, 2, 128, 256), BF),
            D((4,)), D((4, 2)), D((4,)), D,
            D((2, 2, 4)), D((2, 2, 4)), D((5, 2)), D((5, 2)), D((4, 8)), D((4, 8)),
            D((2, 2, 4)), D((2, 2, 4)), D, D,
            D((4, 2)), D((4, 2)), D((4, 2)), D((4, 2)), pltpu.SemaphoreType.REGULAR,
            pltpu.SMEM((1, 1, 2), jnp.int32), D,
        ],
        compiler_params=pltpu.CompilerParams(
            collective_id=0, has_side_effects=True, vmem_limit_bytes=65_000_000
        ),
    )(neighbours, counts, queries, key_states, values, w_out, cotangent)
    return pl.pallas_call(
        flush,
        name="flush",
        out_shape=(big, big, big, big, jax.ShapeDtypeStruct((2, 1024), F32)),
        in_specs=[vmem] * 5,
        out_specs=[hbm] * 5,
        scratch_shapes=[D((5,))],
        compiler_params=pltpu.CompilerParams(vmem_limit_bytes=4_000_000),
    )(*results)


def solution(mesh):
    placed = (
        P("dp", "seq", None),
        P("dp", "seq", None),
        P("dp", "seq", None),
        P(),
        P("dp", "seq", None),
        P("dp", "seq", None),
        P("dp", "seq"),
    )
    return jax.shard_map(
        on_device,
        mesh=mesh,
        in_specs=placed,
        out_specs=(
            P("dp", "seq", None),
            P("dp", "seq", None),
            P("dp", "seq", None),
            P("dp", "seq", None),
            P(("seq", "dp"), None),
        ),
        check_vma=False,
    )
```
